32 devices in a mesh: vol: 2 (over x), row: 16 (over z, y, core).
Axes of the slice: x: 2, y: 2, z: 4, core: 2. Of those that a mesh axis runs over, the one named last changes fastest.
Arguments:
- volume: float32 [6, 2048, 2048], P('vol', 'row'), parts along dimension 0, may hold values from 0.25 to 2
- psf_spectra: bfloat16 [2, 3, 2048, 2048], P(None, None, 'row'), may hold values from -3.5 to 3.5
- background: float32 [2048, 2048], P('row'), may hold values from 1 to 4
- measured: float32 [4096, 2048], P(('vol', 'row')), parts along dimension 0, may hold values from 0.5 to 4
Outputs:
- new_volume: float32 [6, 2048, 2048], P('vol', 'row'), parts along dimension 0
- projection: float32 [4096, 2048], P(('vol', 'row')), parts along dimension 0
The draws below stay inside these ranges and needn't reach their ends.
There are 2 independent parts, one for each index of `vol`. The reference program is written for one: setup_inputs(seed, part) draws one part's arguments, and reference() takes and returns one part's arrays. A program takes and returns all parts, laid end to end along the dimension named above; an argument that names none is the same for every part. Nothing has to cross between parts.
All inputs are finite; a program needn't handle non-finite values.
Results may differ from the reference program's by a relative error of at most 0.0003.
Values sent between devices are 32-bit elements; how exact they have to be, the bound alone decides.
No kernel may reach another device: no remote copies, remote signals or barrier semaphores. Data moves between devices by JAX's collectives and lax.ppermute only.
A program may use at most 128 MiB of HBM per device.

```python
import math
import jax
import jax.numpy as jnp
from jax import lax

SENSOR = 2048
DEPTHS = 3


def shard_levels(own_key, dims, cuts, least, high):
    loudness = 1.0
    for dim, blocks in cuts:
        heights = jax.random.uniform(jax.random.fold_in(jax.random.fold_in(own_key, 6), dim), (blocks,), jnp.float32, least / len(cuts), high / len(cuts))
        loudness = loudness * jnp.repeat(jnp.exp(heights), dims[dim] // blocks).reshape((-1,) + (1,) * (len(dims) - 1 - dim))
    return loudness


def centred(own_key, extent, deviation, most, cuts=(), kind=jnp.bfloat16):
    array = jax.random.normal(own_key, extent, jnp.float32) * deviation
    if len(cuts) > 0:
        array = shard_levels(own_key, extent, cuts, -0.22, 0.18) * array
    return jnp.clip(array, min=-most, max=most).astype(kind)


def setup_inputs(seed: int = 0, part: int = 0) -> dict:
    seeds = jax.random.split(jax.random.key(seed), 5)
    own_keys = jax.random.split(jax.random.fold_in(seeds[4], part), 5)
    volume = jnp.clip(jnp.exp(math.log(2.0) - 2.0794415 * jax.random.uniform(own_keys[0], (DEPTHS, SENSOR, SENSOR), jnp.float32) ** shard_levels(own_keys[0], (DEPTHS, SENSOR, SENSOR), ((1, 16),), -0.2, 0.2)), 0.25, 2.0)
    psf_spectra = centred(seeds[1], (2, DEPTHS, SENSOR, SENSOR), DEPTHS ** -0.5, 3.5, ((2, 16),))
    background = jnp.clip(jnp.exp(math.log(4.0) - 1.3862944 * jax.random.uniform(seeds[2], (SENSOR, SENSOR), jnp.float32) ** shard_levels(seeds[2], (SENSOR, SENSOR), ((0, 16),), -0.2, 0.2)), 1.0, 4.0)
    measured = jnp.clip(jnp.exp(math.log(4.0) - 2.0794415 * jax.random.uniform(own_keys[3], (SENSOR, SENSOR), jnp.float32) ** shard_levels(own_keys[3], (SENSOR, SENSOR), ((0, 16),), -0.2, 0.2)), 0.5, 4.0)
    return {"volume": volume, "psf_spectra": psf_spectra, "background": background, "measured": measured}


FLOOR = 0.5


def reference(volume, psf_spectra, background, measured):
    response = psf_spectra[0].astype(jnp.float32) + 1j * psf_spectra[1].astype(jnp.float32)
    response = jnp.swapaxes(response, 1, 2)

    def project_slice(carry, pieces):
        layer, kernel = pieces
        return carry + jnp.fft.fft2(layer) * kernel, 0

    initial = jnp.zeros(volume.shape[1:], response.dtype)
    summed, unused = lax.scan(project_slice, initial, (volume, response))
    projection = jnp.real(jnp.fft.ifft2(summed)).astype(jnp.float32)
    quotient = measured / jnp.maximum(projection + background, FLOOR)
    quotient_spec = jnp.fft.fft2(quotient)

    def correct_slice(pieces):
        layer, kernel = pieces
        back = jnp.real(jnp.fft.ifft2(quotient_spec * jnp.conj(kernel))).astype(jnp.float32)
        return layer * back

    new_volume = lax.map(correct_slice, (volume, response))
    return new_volume, projection
```

```python
import math

import jax
import jax.numpy as jnp
import numpy as np
from jax import lax
from jax.experimental import pallas as pl
from jax.experimental.pallas import tpu as pltpu
from jax.sharding import PartitionSpec as P

FLOOR = 0.5
HIGHEST = lax.Precision.HIGHEST
LANES = 128
SUB = 8


def phase_pair(first_extent, second_extent, modulus, direction):
    first_idx = jnp.arange(first_extent, dtype=jnp.int32)
    second_idx = jnp.arange(second_extent, dtype=jnp.int32)
    phases = first_idx[:, None] * second_idx[None, :] % modulus
    angles = phases.astype(jnp.float32) * (2.0 * math.pi / modulus)
    return (jnp.cos(angles), direction * jnp.sin(angles))


def contract(pattern, fields, coeffs, real_only):
    real_part, imag_part = fields
    coeff_real, coeff_imag = coeffs

    def product(operand, table_side):
        return jnp.einsum(pattern, operand, table_side, precision=HIGHEST)

    if imag_part is None:
        return (product(real_part, coeff_real), product(real_part, coeff_imag))
    out_real = product(real_part, coeff_real) - product(imag_part, coeff_imag)
    if real_only:
        return (out_real, None)
    return (out_real, product(real_part, coeff_imag) + product(imag_part, coeff_real))


def rotate(fields, factors):
    real_part, imag_part = fields
    factor_real, factor_imag = factors
    return (
        real_part * factor_real - imag_part * factor_imag,
        real_part * factor_imag + imag_part * factor_real,
    )


def leading_pass(fields, groups, direction):
    batch_size, row_count, length = fields[0].shape
    inner_count = length // groups
    shaped = tuple(
        None if member is None else member.reshape(batch_size, row_count, inner_count, groups)
        for member in fields
    )
    sectioned = contract(
        "bqnm,nk->bqkm", shaped, phase_pair(inner_count, inner_count, inner_count, direction), False
    )
    sectioned = rotate(sectioned, phase_pair(inner_count, groups, length, direction))
    sectioned = contract(
        "bqkm,mp->bpkq", sectioned, phase_pair(groups, groups, groups, direction), False
    )
    return tuple(member.reshape(batch_size, groups, inner_count * row_count) for member in sectioned)


def trailing_pass(fields, row_count, direction, real_only):
    batch_size, groups, merged = fields[0].shape
    inner_count = merged // row_count
    length = groups * row_count
    shaped = tuple(member.reshape(batch_size, groups, inner_count, row_count) for member in fields)
    sectioned = contract(
        "bskq,st->bktq", shaped, phase_pair(groups, groups, groups, direction), False
    )
    sectioned = rotate(sectioned, phase_pair(groups, row_count, length, direction))
    sectioned = contract(
        "bktq,qu->bkut", sectioned, phase_pair(row_count, row_count, row_count, direction), real_only
    )
    return tuple(
        None if member is None else member.reshape(batch_size, inner_count, length)
        for member in sectioned
    )


def generic_shards(volume, psf_spectra, background, measured):
    groups = lax.axis_size("row")
    row_count = volume.shape[1]
    length = volume.shape[2]
    inverse_scale = 1.0 / (length * length)
    response_real = psf_spectra[0].astype(jnp.float32)
    response_imag = psf_spectra[1].astype(jnp.float32)

    def swap(field):
        return lax.all_to_all(field, "row", split_axis=1, concat_axis=1, tiled=True)

    outgoing = leading_pass((volume, None), groups, -1.0)
    spec_real, spec_imag = trailing_pass(
        (swap(outgoing[0]), swap(outgoing[1])), row_count, -1.0, False
    )
    prod_real = spec_real * response_real - spec_imag * response_imag
    prod_imag = spec_real * response_imag + spec_imag * response_real
    summed = (jnp.sum(prod_real, axis=0, keepdims=True), jnp.sum(prod_imag, axis=0, keepdims=True))
    outgoing = leading_pass(summed, groups, 1.0)
    arrived = (swap(outgoing[0]), swap(outgoing[1]))
    projection = trailing_pass(arrived, row_count, 1.0, True)[0][0] * inverse_scale
    quotient = measured / jnp.maximum(projection + background, FLOOR)
    outgoing = leading_pass((quotient[None], None), groups, -1.0)
    arrived = (swap(outgoing[0]), swap(outgoing[1]))
    ratio_real, ratio_imag = trailing_pass(arrived, row_count, -1.0, False)
    corr_real = ratio_real * response_real + ratio_imag * response_imag
    corr_imag = ratio_imag * response_real - ratio_real * response_imag
    outgoing = leading_pass((corr_real, corr_imag), groups, 1.0)
    arrived = (swap(outgoing[0]), swap(outgoing[1]))
    correction = trailing_pass(arrived, row_count, 1.0, True)[0] * inverse_scale
    return (volume * correction, projection)


def times(z, angle):
    re, im = z
    c, s = math.cos(angle), math.sin(angle)
    if abs(s) < 1e-12:
        return z if c > 0 else (-re, None if im is None else -im)
    if abs(c) < 1e-12:
        if im is None:
            return (None, re if s > 0 else -re)
        return (-im, re) if s > 0 else (im, -re)
    if im is None:
        return (re * c, re * s)
    if abs(abs(c) - abs(s)) < 1e-12:
        sc, ss = math.copysign(1.0, c), math.copysign(1.0, s)
        a = re if sc > 0 else -re
        b = im if sc > 0 else -im
        r, i = (a - im, b + re) if ss > 0 else (a + im, b - re)
        return (r * abs(c), i * abs(c))
    return (re * c - im * s, re * s + im * c)


def plus(a, b):
    if a is None:
        return b
    return a if b is None else a + b


def minus(a, b):
    if b is None:
        return a
    return -b if a is None else a - b


def cadd(a, b):
    return (plus(a[0], b[0]), plus(a[1], b[1]))


def csub(a, b):
    return (minus(a[0], b[0]), minus(a[1], b[1]))


def conj(a):
    return (a[0], None if a[1] is None else -a[1])


def cfft(xs, sign):
    n = len(xs)
    if n == 1:
        return list(xs)
    even, odd = cfft(xs[0::2], sign), cfft(xs[1::2], sign)
    turned = [times(odd[t], sign * 2.0 * math.pi * t / n) for t in range(n // 2)]
    return [cadd(even[t], turned[t]) for t in range(n // 2)] + [
        csub(even[t], turned[t]) for t in range(n // 2)
    ]


def rfft(xs):
    n = len(xs)
    if n == 2:
        return [(xs[0] + xs[1], None), (xs[0] - xs[1], None)]
    even, odd = rfft(xs[0::2]), rfft(xs[1::2])
    out = [None] * (n // 2 + 1)
    for t in range(n // 4 + 1):
        turned = times(odd[t], -2.0 * math.pi * t / n)
        out[t] = cadd(even[t], turned)
        if t < n // 4:
            out[n // 2 - t] = conj(csub(even[t], turned))
    return out


def c2r(zs):
    n = 2 * (len(zs) - 1)
    if n == 2:
        return [zs[0][0] + zs[1][0], zs[0][0] - zs[1][0]]
    q = n // 4
    even, odd = [], []
    for t in range(q):
        mirror = conj(zs[n // 2 - t])
        even.append(cadd(zs[t], mirror))
        odd.append(times(csub(zs[t], mirror), 2.0 * math.pi * t / n))
    even.append((zs[q][0] * 2.0, None))
    odd.append((zs[q][1] * -2.0, None))
    a, b = c2r(even), c2r(odd)
    return [half[i] for i in range(n // 2) for half in (a, b)]


def split_table(table):
    high = table.astype(jnp.bfloat16)
    low = (table - high.astype(np.float64)).astype(jnp.bfloat16)
    return np.stack([high, low])


def make_tables(groups, lanes):
    length = groups * lanes
    per = lanes // groups
    pos = np.arange(lanes)
    w_y = np.zeros((groups, 2, SUB, 2, lanes))
    w_0 = np.zeros((groups, 2, SUB, 2, lanes))
    half = SUB // 2
    for p in range(groups):
        for r in range(SUB):
            ang = 2.0 * np.pi * ((per * p + r) * pos % lanes) / lanes
            w_y[p, 0, r] = np.cos(ang), np.sin(ang)
            w_y[p, 1, r] = -np.sin(ang), np.cos(ang)
            if r < half:
                unit = per * p + r
                if r == 0 and p >= groups // 2:
                    unit = per * p + per // 2
                ang = 2.0 * np.pi * (groups * unit * pos % length) / length
                w_0[p, 0, r, 0] = np.cos(ang)
                w_0[p, 1, r, 0] = -np.sin(ang)
                if r == 0 and p == 0:
                    w_0[p, 1, r, 0] = (-1.0) ** pos
            else:
                ang = (groups * (per * p + r - half) + groups // 2) * pos % length
                ang = 2.0 * np.pi * ang / length
                w_0[p, 0, r, 1] = np.cos(ang)
                w_0[p, 1, r, 1] = -np.sin(ang)
    rows = groups * 2 * SUB
    ang = 2.0 * np.pi * (pos[:, None] * pos[None, :] % lanes) / lanes
    w_x = np.block([[np.cos(ang), -np.sin(ang)], [np.sin(ang), np.cos(ang)]])
    ang = 2.0 * np.pi * (np.arange(groups)[:, None] * pos[None, :] % length) / length
    turn = np.stack([np.cos(ang), -np.sin(ang)], axis=1).astype(np.float32)
    return (
        split_table(w_y.reshape(rows, 2 * lanes)),
        split_table(w_0.reshape(rows, 2 * lanes)),
        split_table(w_x),
        split_table(w_x.T),
        turn,
    )


def kept_rows(groups, lanes):
    per = lanes // groups
    half = SUB // 2
    own = [groups * w for w in range(half)] + [groups * w + groups // 2 for w in range(half)]
    for tile in range(1, groups // 2):
        own += [groups * w + tile for w in range(per)]
    return own


NN = (((1,), (0,)), ((), ()))
NT = (((1,), (1,)), ((), ()))


def halves(x):
    high = x.astype(jnp.bfloat16)
    return high, (x - high.astype(jnp.float32)).astype(jnp.bfloat16)


def mm(a, b, dims):
    return lax.dot_general(a, b, dims, preferred_element_type=jnp.float32)


def data_table(x, table):
    high, low = halves(x)
    return mm(high, table[0], NN) + (mm(low, table[0], NN) + mm(high, table[1], NN))


def table_data(table, x):
    high, low = halves(x)
    return mm(table[0], high, NT) + (mm(table[0], low, NT) + mm(table[1], high, NT))


def y_forward(read, emit, z, w_y, w_0, turn, groups, rows, lanes):
    def chunk(i, carry):
        out = rfft([read(i, a) for a in range(groups)])
        here = pl.ds(pl.multiple_of(i * SUB, SUB), SUB)
        z[0, here, :lanes] = out[0][0]
        z[0, here, lanes:] = out[groups // 2][0]
        for t in range(1, groups // 2):
            re, im = out[t]
            c, s = turn[t, 0:1, :], turn[t, 1:2, :]
            z[t, here, :lanes] = re * c - im * s
            z[t, here, lanes:] = re * s + im * c
        return carry

    lax.fori_loop(0, rows // SUB, chunk, 0)
    for t in range(groups // 2):
        emit(t, table_data(w_0 if t == 0 else w_y, z[t]))


def y_inverse(fetch, write, z, w_y, w_0, turn, groups, rows, lanes):
    for t in range(groups // 2):
        z[t] = data_table(fetch(t).T, w_0 if t == 0 else w_y)

    def chunk(i, carry):
        here = pl.ds(pl.multiple_of(i * SUB, SUB), SUB)
        zs = [(z[0, here, :lanes] * 2.0, None)]
        for t in range(1, groups // 2):
            re, im = z[t, here, :lanes], z[t, here, lanes:]
            c, s = turn[t, 0:1, :], turn[t, 1:2, :]
            zs.append((re * c + im * s, im * c - re * s))
        zs.append((z[0, here, lanes:] * 2.0, None))
        write(i, here, c2r(zs))
        return carry

    lax.fori_loop(0, rows // SUB, chunk, 0)


def x_radix(tile, z, base, turn, groups, lanes, step):
    for t, (re, im) in enumerate(cfft(tile, -1.0)):
        here = pl.ds(pl.multiple_of(base + t * step, SUB), SUB)
        if t == 0:
            z[here, :lanes] = re
            z[here, lanes:] = im
        else:
            c, s = turn[t, 0:1, :], turn[t, 1:2, :]
            z[here, :lanes] = re * c - im * s
            z[here, lanes:] = re * s + im * c


def x_unradix(z, base, turn, groups, lanes, step):
    zs = []
    for t in range(groups):
        here = pl.ds(pl.multiple_of(base + t * step, SUB), SUB)
        re, im = z[here, :lanes], z[here, lanes:]
        if t:
            c, s = turn[t, 0:1, :], turn[t, 1:2, :]
            re, im = re * c + im * s, im * c - re * s
        zs.append((re, im))
    return cfft(zs, 1.0)


def fast_shards(volume, psf_spectra, background, measured):
    groups = lax.axis_size("row")
    parts = lax.axis_size("vol")
    depth, rows, length = volume.shape
    lanes = LANES
    tiles = groups // 2
    kept = tiles * SUB
    pair = 2 * SUB
    f32 = jnp.float32
    place = lax.axis_index("row")
    part = lax.axis_index("vol")
    w_y, w_0, w_x, w_xi, turn = (jnp.asarray(t) for t in make_tables(groups, lanes))
    own_rows = kept_rows(groups, rows)

    whole = lambda *shape: pl.BlockSpec(shape, lambda *_: (0,) * len(shape))
    y_specs = [whole(*w_y.shape), whole(*w_0.shape), whole(*turn.shape)]
    x_specs = [whole(*w_x.shape), whole(*w_xi.shape), whole(*turn.shape)]
    y_scratch = pltpu.VMEM((tiles, rows, 2 * lanes), f32)
    send_shape = (groups, tiles, 2, SUB, lanes)

    def many(n):
        return (groups, n, tiles, 2, SUB, lanes)

    low = place < groups // 2
    mid = rows // 2
    pick_send = np.zeros((kept, rows), np.float32)
    pick_own = np.zeros((kept, rows), np.float32)
    for r, k in enumerate(own_rows):
        pick_send[r, (rows - k) if k else mid] = 1.0
        pick_own[r, k] = 1.0
    pick_high = pick_own.copy()
    pick_high[0] = 0.0
    pick_high[0, mid] = 1.0

    def pick_kernel(where_ref, sel_ref, own_l_ref, own_h_ref, psf_ref, send_ref, own_ref):
        sel = jnp.where(where_ref[0] == 1, own_l_ref[...], own_h_ref[...])
        for c in range(2):
            own_ref[c, 0] = mm(sel, psf_ref[c, 0], NN)

        @pl.when(where_ref[1] == 0)
        def _():
            send_ref[0] = mm(sel_ref[...], psf_ref[0, 0], NN)

        @pl.when(where_ref[1] != 0)
        def _():
            send_ref[0] = mm(sel_ref[...], psf_ref[1, 0], NN)

    flags = jnp.stack([low.astype(jnp.int32), part.astype(jnp.int32), (place == 0).astype(jnp.int32)])
    smem = pl.BlockSpec(memory_space=pltpu.SMEM)
    bf = jnp.bfloat16
    send, own = pl.pallas_call(
        pick_kernel,
        grid=(depth,),
        in_specs=[smem, whole(kept, rows), whole(kept, rows), whole(kept, rows),
                  pl.BlockSpec((2, 1, rows, length), lambda d: (0, d, 0, 0))],
        out_specs=[pl.BlockSpec((1, kept, length), lambda d: (d, 0, 0)),
                   pl.BlockSpec((2, 1, kept, length), lambda d: (0, d, 0, 0))],
        out_shape=[jax.ShapeDtypeStruct((depth, kept, length), f32),
                   jax.ShapeDtypeStruct((2, depth, kept, length), f32)],
        name="pick",
    )(flags, jnp.asarray(pick_send, bf), jnp.asarray(pick_own, bf), jnp.asarray(pick_high, bf), psf_spectra)
    flip = [(p, groups - 1 - p) for p in range(groups)]
    mine = lax.ppermute(send, "row", flip)
    other = lax.ppermute(mine, "vol", [(0, 1), (1, 0)])
    edge = psf_spectra[:, :, 0, :].astype(f32).reshape(2 * depth, length)
    edge = jnp.pad(edge, ((0, pair - 2 * depth), (0, 0)))
    edge = lax.ppermute(edge, "row", [(groups - p, p) for p in range(1, groups // 2)] + [(groups // 2, 0)])

    scale = 0.5 / (length * length)
    many_t = 2
    width = many_t * lanes

    def mix_kernel(where_ref, own_ref, mine_ref, other_ref, edge_ref, a_ref, b_ref, o_s, p_s, e_s):
        step = pl.program_id(0)

        @pl.when(step == 0)
        def _():
            zero = where_ref[2] == 1
            is_low = where_ref[0] == 1
            first = lax.broadcasted_iota(jnp.int32, (SUB, length), 0) == 0
            for c in range(2):
                for d in range(depth):
                    base = (c * depth + d) * kept
                    mine_here = where_ref[1] == c
                    o_s[base:base + kept, :] = own_ref[c, d].astype(bf)
                    p = jnp.where(mine_here, mine_ref[d], other_ref[d])
                    row = c * depth + d
                    swap = jnp.where(zero, own_ref[c, d, 0:1, :], edge_ref[row:row + 1, :])
                    head = jnp.where(jnp.logical_and(first, is_low), swap, p[:SUB])
                    p_s[base:base + kept, :] = jnp.concatenate([head, p[SUB:]], 0).astype(bf)
            e_s[...] = edge_ref[...].astype(bf)

        freq = lax.broadcasted_iota(jnp.int32, (length, width), 0)
        col = lax.broadcasted_iota(jnp.int32, (length, width), 1)
        target = (col % lanes) * groups + step * many_t + col // lanes
        hot = jnp.where(freq == target, 1.0, 0.0).astype(bf)
        hot_rev = jnp.where(freq == (length - target) % length, 1.0, 0.0).astype(bf)
        plain = mm(o_s[...], hot, NN)
        mirror = mm(p_s[...], hot_rev, NN)
        e_plain = mm(e_s[...], hot, NN)
        e_mirror = mm(e_s[...], hot_rev, NN)
        zero = jnp.where(where_ref[2] == 1, 1.0, 0.0).astype(f32)
        first = lax.broadcasted_iota(jnp.int32, (SUB, width), 0) == 0
        for c in range(2):
            sign = 1.0 if c == 0 else -1.0
            for d in range(depth):
                row = c * depth + d
                base = row * kept
                h = (plain[base:base + kept] + sign * mirror[base:base + kept]) * scale
                e = (e_plain[row:row + 1] + sign * e_mirror[row:row + 1]) * scale
                a0 = h[:SUB] * (1.0 - 0.75 * zero) + (0.25 * zero) * e
                b0 = (h[:SUB] - e) * (0.25 * zero)
                a_ref[c, d, :SUB, :] = jnp.where(first, a0, h[:SUB])
                a_ref[c, d, SUB:, :] = h[SUB:]
                b_ref[c, d, :SUB, :] = jnp.where(first, b0, 0.0)
                b_ref[c, d, SUB:, :] = jnp.zeros((SUB, width), f32)

    planes = 2 * depth * kept
    a_all, b_all = pl.pallas_call(
        mix_kernel,
        grid=(groups // many_t,),
        in_specs=[smem, whole(2, depth, kept, length), whole(depth, kept, length),
                  whole(depth, kept, length), whole(pair, length)],
        out_specs=[pl.BlockSpec((2, depth, kept, width), lambda i: (0, 0, 0, i)),
                   pl.BlockSpec((2, depth, pair, width), lambda i: (0, 0, 0, i))],
        out_shape=[jax.ShapeDtypeStruct((2, depth, kept, length), f32),
                   jax.ShapeDtypeStruct((2, depth, pair, length), f32)],
        scratch_shapes=[pltpu.VMEM((planes, length), bf), pltpu.VMEM((planes, length), bf),
                        pltpu.VMEM((pair, length), bf)],
        name="mix",
    )(flags, own, mine, other, edge)

    def forward_kernel(wy_ref, w0_ref, turn_ref, v_ref, o_ref, z):
        def read(i, a):
            return v_ref[0, pl.ds(pl.multiple_of(i * SUB, SUB), SUB), a * lanes:(a + 1) * lanes]

        def emit(t, out):
            o_ref[:, 0, t] = out.reshape(groups, 2, SUB, rows)

        y_forward(read, emit, z, wy_ref, w0_ref, turn_ref, groups, rows, lanes)

    outgoing = pl.pallas_call(
        forward_kernel,
        grid=(depth,),
        in_specs=y_specs + [pl.BlockSpec((1, rows, length), lambda d: (d, 0, 0))],
        out_specs=pl.BlockSpec((groups, 1, tiles, 2, SUB, lanes), lambda d: (0, d, 0, 0, 0, 0)),
        out_shape=jax.ShapeDtypeStruct(many(depth), f32),
        scratch_shapes=[y_scratch],
        name="forward_y",
    )(w_y, w_0, turn, volume)

    def swap(field):
        return lax.all_to_all(field, "row", split_axis=0, concat_axis=0, tiled=True)

    arrived = swap(outgoing)

    block = groups * pair
    x_scratch = lambda n: pltpu.VMEM((n * block, 2 * lanes), f32)

    def source(s_ref, d, h, flipped=False):
        out = []
        for s in range(groups):
            re, im = s_ref[s, d, h, 0], s_ref[s, d, h, 1]
            out.append((re, -im if flipped else im))
        return out

    def project_kernel(wx_ref, wxi_ref, turn_ref, s_ref, a_ref, b_ref, o_ref, z, t_s, zc):
        def gather(flipped):
            def one(i, carry):
                d, h = i // 2, i % 2
                x_radix(source(s_ref, d, h, flipped), z, d * block + h * SUB, turn_ref, groups, lanes, pair)
                return carry
            lax.fori_loop(0, 2 * depth, one, 0)
            for d in range(depth):
                zc[d * block:(d + 1) * block, :] = data_table(z[d * block:(d + 1) * block, :], wx_ref)

        def multiply(k_ref, fresh):
            for t in range(groups):
                here = slice(t * pair, (t + 1) * pair)
                cols = slice(t * lanes, (t + 1) * lanes)
                re, im = (None, None) if fresh else (t_s[here, :lanes], t_s[here, lanes:])
                for d in range(depth):
                    at = slice(d * block + t * pair, d * block + (t + 1) * pair)
                    zr, zi = zc[at, :lanes], zc[at, lanes:]
                    kr, ki = k_ref[0, d, :, cols], k_ref[1, d, :, cols]
                    re = plus(re, zr * kr - zi * ki)
                    im = plus(im, zr * ki + zi * kr)
                t_s[here, :lanes] = re
                t_s[here, lanes:] = im

        gather(False)
        multiply(a_ref, True)

        @pl.when(pl.program_id(0) == 0)
        def _():
            gather(True)
            multiply(b_ref, False)

        zc[:block, :] = data_table(t_s[...], wxi_ref)

        def back(h, carry):
            for s, (re, im) in enumerate(x_unradix(zc, h * SUB, turn_ref, groups, lanes, pair)):
                o_ref[s, h, 0] = re
                o_ref[s, h, 1] = im
            return carry
        lax.fori_loop(0, 2, back, 0)

    k_specs = [pl.BlockSpec((2, depth, pair, length), lambda j: (0, 0, j, 0)),
               whole(2, depth, pair, length)]
    one_spec = pl.BlockSpec((groups, 2, 2, SUB, lanes), lambda j: (0, j, 0, 0, 0))
    all_spec = pl.BlockSpec((groups, depth, 2, 2, SUB, lanes), lambda j: (0, 0, j, 0, 0, 0))
    outgoing = pl.pallas_call(
        project_kernel,
        grid=(tiles // 2,),
        in_specs=x_specs + [all_spec] + k_specs,
        out_specs=one_spec,
        out_shape=jax.ShapeDtypeStruct(send_shape, f32),
        scratch_shapes=[x_scratch(depth), x_scratch(1), x_scratch(depth)],
        name="project_x",
    )(w_x, w_xi, turn, arrived, a_all, b_all)
    arrived = swap(outgoing)

    def ratio_kernel(wy_ref, w0_ref, turn_ref, g_ref, bg_ref, me_ref, p_ref, o_ref, z, q_s):
        def fetch(t):
            return g_ref[:, t].reshape(groups * 2 * SUB, rows)

        def write(i, here, outs):
            for a, value in enumerate(outs):
                cols = slice(a * lanes, (a + 1) * lanes)
                p_ref[here, cols] = value
                q_s[here, cols] = me_ref[here, cols] / jnp.maximum(value + bg_ref[here, cols], FLOOR)

        y_inverse(fetch, write, z, wy_ref, w0_ref, turn_ref, groups, rows, lanes)

        def read(i, a):
            return q_s[pl.ds(pl.multiple_of(i * SUB, SUB), SUB), a * lanes:(a + 1) * lanes]

        def emit(t, out):
            o_ref[:, t] = out.reshape(groups, 2, SUB, rows)

        y_forward(read, emit, z, wy_ref, w0_ref, turn_ref, groups, rows, lanes)

    projection, outgoing = pl.pallas_call(
        ratio_kernel,
        out_shape=[jax.ShapeDtypeStruct((rows, length), f32), jax.ShapeDtypeStruct(send_shape, f32)],
        scratch_shapes=[y_scratch, pltpu.VMEM((rows, length), f32)],
        name="ratio",
    )(w_y, w_0, turn, arrived, background, measured)
    arrived = swap(outgoing)

    def correct_kernel(wx_ref, wxi_ref, turn_ref, s_ref, a_ref, b_ref, o_ref, z, zq, zc, c_s):
        def gather(flipped, out):
            def one(h, carry):
                tile = []
                for s in range(groups):
                    re, im = s_ref[s, h, 0], s_ref[s, h, 1]
                    tile.append((re, -im if flipped else im))
                x_radix(tile, z, h * SUB, turn_ref, groups, lanes, pair)
                return carry
            lax.fori_loop(0, 2, one, 0)
            out[...] = data_table(z[...], wx_ref)

        def multiply(k_ref, src, fresh):
            for t in range(groups):
                here = slice(t * pair, (t + 1) * pair)
                cols = slice(t * lanes, (t + 1) * lanes)
                zr, zi = src[here, :lanes], src[here, lanes:]
                for d in range(depth):
                    at = slice(d * block + t * pair, d * block + (t + 1) * pair)
                    kr, ki = k_ref[0, d, :, cols], k_ref[1, d, :, cols]
                    re, im = zr * kr + zi * ki, zi * kr - zr * ki
                    if not fresh:
                        re, im = re + c_s[at, :lanes], im + c_s[at, lanes:]
                    c_s[at, :lanes] = re
                    c_s[at, lanes:] = im

        gather(False, zq)
        multiply(a_ref, zq, True)

        @pl.when(pl.program_id(0) == 0)
        def _():
            gather(True, zq)
            multiply(b_ref, zq, False)

        for d in range(depth):
            zc[d * block:(d + 1) * block, :] = data_table(c_s[d * block:(d + 1) * block, :], wxi_ref)

        def back(i, carry):
            d, h = i // 2, i % 2
            out = x_unradix(zc, d * block + h * SUB, turn_ref, groups, lanes, pair)
            for s, (re, im) in enumerate(out):
                o_ref[s, d, h, 0] = re
                o_ref[s, d, h, 1] = im
            return carry
        lax.fori_loop(0, 2 * depth, back, 0)

    outgoing = pl.pallas_call(
        correct_kernel,
        grid=(tiles // 2,),
        in_specs=x_specs + [one_spec] + k_specs,
        out_specs=all_spec,
        out_shape=jax.ShapeDtypeStruct(many(depth), f32),
        scratch_shapes=[x_scratch(1), x_scratch(1), x_scratch(depth), x_scratch(depth)],
        name="correct_x",
    )(w_x, w_xi, turn, arrived, a_all, b_all)
    arrived = swap(outgoing)

    def final_kernel(wy_ref, w0_ref, turn_ref, g_ref, v_ref, o_ref, z):
        def fetch(t):
            return g_ref[:, 0, t].reshape(groups * 2 * SUB, rows)

        def write(i, here, outs):
            for a, value in enumerate(outs):
                cols = slice(a * lanes, (a + 1) * lanes)
                o_ref[0, here, cols] = v_ref[0, here, cols] * value

        y_inverse(fetch, write, z, wy_ref, w0_ref, turn_ref, groups, rows, lanes)

    new_volume = pl.pallas_call(
        final_kernel,
        grid=(depth,),
        in_specs=y_specs + [
            pl.BlockSpec((groups, 1, tiles, 2, SUB, lanes), lambda d: (0, d, 0, 0, 0, 0)),
            pl.BlockSpec((1, rows, length), lambda d: (d, 0, 0))],
        out_specs=pl.BlockSpec((1, rows, length), lambda d: (d, 0, 0)),
        out_shape=jax.ShapeDtypeStruct((depth, rows, length), f32),
        scratch_shapes=[y_scratch],
        name="final_y",
    )(w_y, w_0, turn, arrived, volume)
    return new_volume, projection


def solution(mesh):
    groups, parts = mesh.shape["row"], mesh.shape["vol"]

    def shards(volume, psf_spectra, background, measured):
        rows = volume.shape[1]
        fits = parts == 2 and rows == LANES and rows == SUB * groups
        body = fast_shards if fits else generic_shards
        return body(volume, psf_spectra, background, measured)

    in_specs = (
        P("vol", "row", None),
        P(None, None, "row", None),
        P("row", None),
        P(("vol", "row"), None),
    )
    out_specs = (P("vol", "row", None), P(("vol", "row"), None))
    return jax.shard_map(shards, mesh=mesh, in_specs=in_specs, out_specs=out_specs, check_vma=False)
```

```python
import math

import jax
import jax.numpy as jnp
import numpy as np
from jax import lax
from jax.experimental import pallas as pl
from jax.experimental.pallas import tpu as pltpu
from jax.sharding import PartitionSpec as P


FLOOR = 0.5
HIGHEST = lax.Precision.HIGHEST
LANES = 128
SUB = 8


def phase_pair(first_extent, second_extent, modulus, direction):
    first_idx = jnp.arange(first_extent, dtype=jnp.int32)
    second_idx = jnp.arange(second_extent, dtype=jnp.int32)
    phases = first_idx[:, None] * second_idx[None, :] % modulus
    angles = phases.astype(jnp.float32) * (2.0 * math.pi / modulus)
    return (jnp.cos(angles), direction * jnp.sin(angles))


def contract(pattern, fields, coeffs, real_only):
    real_part, imag_part = fields
    coeff_real, coeff_imag = coeffs

    def product(operand, table_side):
        return jnp.einsum(pattern, operand, table_side, precision=HIGHEST)

    if imag_part is None:
        return (product(real_part, coeff_real), product(real_part, coeff_imag))
    out_real = product(real_part, coeff_real) - product(imag_part, coeff_imag)
    if real_only:
        return (out_real, None)
    return (out_real, product(real_part, coeff_imag) + product(imag_part, coeff_real))


def rotate(fields, factors):
    real_part, imag_part = fields
    factor_real, factor_imag = factors
    return (
        real_part * factor_real - imag_part * factor_imag,
        real_part * factor_imag + imag_part * factor_real,
    )


def leading_pass(fields, groups, direction):
    batch_size, row_count, length = fields[0].shape
    inner_count = length // groups
    shaped = tuple(
        None if member is None else member.reshape(batch_size, row_count, inner_count, groups)
        for member in fields
    )
    sectioned = contract(
        "bqnm,nk->bqkm", shaped, phase_pair(inner_count, inner_count, inner_count, direction), False
    )
    sectioned = rotate(sectioned, phase_pair(inner_count, groups, length, direction))
    sectioned = contract(
        "bqkm,mp->bpkq", sectioned, phase_pair(groups, groups, groups, direction), False
    )
    return tuple(member.reshape(batch_size, groups, inner_count * row_count) for member in sectioned)


def trailing_pass(fields, row_count, direction, real_only):
    batch_size, groups, merged = fields[0].shape
    inner_count = merged // row_count
    length = groups * row_count
    shaped = tuple(member.reshape(batch_size, groups, inner_count, row_count) for member in fields)
    sectioned = contract(
        "bskq,st->bktq", shaped, phase_pair(groups, groups, groups, direction), False
    )
    sectioned = rotate(sectioned, phase_pair(groups, row_count, length, direction))
    sectioned = contract(
        "bktq,qu->bkut", sectioned, phase_pair(row_count, row_count, row_count, direction), real_only
    )
    return tuple(
        None if member is None else member.reshape(batch_size, inner_count, length)
        for member in sectioned
    )


def generic_shards(volume, psf_spectra, background, measured):
    groups = lax.axis_size("row")
    row_count = volume.shape[1]
    length = volume.shape[2]
    inverse_scale = 1.0 / (length * length)
    response_real = psf_spectra[0].astype(jnp.float32)
    response_imag = psf_spectra[1].astype(jnp.float32)

    def swap(field):
        return lax.all_to_all(field, "row", split_axis=1, concat_axis=1, tiled=True)

    outgoing = leading_pass((volume, None), groups, -1.0)
    spec_real, spec_imag = trailing_pass(
        (swap(outgoing[0]), swap(outgoing[1])), row_count, -1.0, False
    )
    prod_real = spec_real * response_real - spec_imag * response_imag
    prod_imag = spec_real * response_imag + spec_imag * response_real
    summed = (jnp.sum(prod_real, axis=0, keepdims=True), jnp.sum(prod_imag, axis=0, keepdims=True))
    outgoing = leading_pass(summed, groups, 1.0)
    arrived = (swap(outgoing[0]), swap(outgoing[1]))
    projection = trailing_pass(arrived, row_count, 1.0, True)[0][0] * inverse_scale
    quotient = measured / jnp.maximum(projection + background, FLOOR)
    outgoing = leading_pass((quotient[None], None), groups, -1.0)
    arrived = (swap(outgoing[0]), swap(outgoing[1]))
    ratio_real, ratio_imag = trailing_pass(arrived, row_count, -1.0, False)
    corr_real = ratio_real * response_real + ratio_imag * response_imag
    corr_imag = ratio_imag * response_real - ratio_real * response_imag
    outgoing = leading_pass((corr_real, corr_imag), groups, 1.0)
    arrived = (swap(outgoing[0]), swap(outgoing[1]))
    correction = trailing_pass(arrived, row_count, 1.0, True)[0] * inverse_scale
    return (volume * correction, projection)


def times(z, angle):
    re, im = z
    c, s = math.cos(angle), math.sin(angle)
    if abs(s) < 1e-12:
        return z if c > 0 else (-re, None if im is None else -im)
    if abs(c) < 1e-12:
        if im is None:
            return (None, re if s > 0 else -re)
        return (-im, re) if s > 0 else (im, -re)
    if im is None:
        return (re * c, re * s)
    if abs(abs(c) - abs(s)) < 1e-12:
        sc, ss = math.copysign(1.0, c), math.copysign(1.0, s)
        a = re if sc > 0 else -re
        b = im if sc > 0 else -im
        r, i = (a - im, b + re) if ss > 0 else (a + im, b - re)
        return (r * abs(c), i * abs(c))
    return (re * c - im * s, re * s + im * c)


def plus(a, b):
    if a is None:
        return b
    return a if b is None else a + b


def minus(a, b):
    if b is None:
        return a
    return -b if a is None else a - b


def cadd(a, b):
    return (plus(a[0], b[0]), plus(a[1], b[1]))


def csub(a, b):
    return (minus(a[0], b[0]), minus(a[1], b[1]))


def conj(a):
    return (a[0], None if a[1] is None else -a[1])


def cfft(xs, sign):
    n = len(xs)
    if n == 1:
        return list(xs)
    even, odd = cfft(xs[0::2], sign), cfft(xs[1::2], sign)
    turned = [times(odd[t], sign * 2.0 * math.pi * t / n) for t in range(n // 2)]
    return [cadd(even[t], turned[t]) for t in range(n // 2)] + [
        csub(even[t], turned[t]) for t in range(n // 2)
    ]


def rfft(xs):
    n = len(xs)
    if n == 2:
        return [(xs[0] + xs[1], None), (xs[0] - xs[1], None)]
    even, odd = rfft(xs[0::2]), rfft(xs[1::2])
    out = [None] * (n // 2 + 1)
    for t in range(n // 4 + 1):
        turned = times(odd[t], -2.0 * math.pi * t / n)
        out[t] = cadd(even[t], turned)
        if t < n // 4:
            out[n // 2 - t] = conj(csub(even[t], turned))
    return out


def c2r(zs):
    n = 2 * (len(zs) - 1)
    if n == 2:
        return [zs[0][0] + zs[1][0], zs[0][0] - zs[1][0]]
    q = n // 4
    even, odd = [], []
    for t in range(q):
        mirror = conj(zs[n // 2 - t])
        even.append(cadd(zs[t], mirror))
        odd.append(times(csub(zs[t], mirror), 2.0 * math.pi * t / n))
    even.append((zs[q][0] * 2.0, None))
    odd.append((zs[q][1] * -2.0, None))
    a, b = c2r(even), c2r(odd)
    return [half[i] for i in range(n // 2) for half in (a, b)]


def split_table(table):
    high = table.astype(jnp.bfloat16)
    low = (table - high.astype(np.float64)).astype(jnp.bfloat16)
    return np.stack([high, low])


def make_tables(groups, lanes):
    length = groups * lanes
    per = lanes // groups
    pos = np.arange(lanes)
    w_y = np.zeros((groups, 2, SUB, 2, lanes))
    w_0 = np.zeros((groups, 2, SUB, 2, lanes))
    half = SUB // 2
    for p in range(groups):
        for r in range(SUB):
            ang = 2.0 * np.pi * ((per * p + r) * pos % lanes) / lanes
            w_y[p, 0, r] = np.cos(ang), np.sin(ang)
            w_y[p, 1, r] = -np.sin(ang), np.cos(ang)
            if r < half:
                unit = per * p + r
                if r == 0 and p >= groups // 2:
                    unit = per * p + per // 2
                ang = 2.0 * np.pi * (groups * unit * pos % length) / length
                w_0[p, 0, r, 0] = np.cos(ang)
                w_0[p, 1, r, 0] = -np.sin(ang)
                if r == 0 and p == 0:
                    w_0[p, 1, r, 0] = (-1.0) ** pos
            else:
                ang = (groups * (per * p + r - half) + groups // 2) * pos % length
                ang = 2.0 * np.pi * ang / length
                w_0[p, 0, r, 1] = np.cos(ang)
                w_0[p, 1, r, 1] = -np.sin(ang)
    rows = groups * 2 * SUB
    ang = 2.0 * np.pi * (pos[:, None] * pos[None, :] % lanes) / lanes
    w_x = np.block([[np.cos(ang), -np.sin(ang)], [np.sin(ang), np.cos(ang)]])
    ang = 2.0 * np.pi * (np.arange(groups)[:, None] * pos[None, :] % length) / length
    turn = np.stack([np.cos(ang), -np.sin(ang)], axis=1).astype(np.float32)
    return (
        split_table(w_y.reshape(rows, 2 * lanes)),
        split_table(w_0.reshape(rows, 2 * lanes)),
        split_table(w_x),
        split_table(w_x.T),
        turn,
    )


def kept_rows(groups, lanes):
    per = lanes // groups
    half = SUB // 2
    own = [groups * w for w in range(half)] + [groups * w + groups // 2 for w in range(half)]
    for tile in range(1, groups // 2):
        own += [groups * w + tile for w in range(per)]
    return own


NN = (((1,), (0,)), ((), ()))
NT = (((1,), (1,)), ((), ()))


def halves(x):
    high = x.astype(jnp.bfloat16)
    return high, (x - high.astype(jnp.float32)).astype(jnp.bfloat16)


def mm(a, b, dims):
    return lax.dot_general(a, b, dims, preferred_element_type=jnp.float32)


def data_table(x, table):
    high, low = halves(x)
    return mm(high, table[0], NN) + (mm(low, table[0], NN) + mm(high, table[1], NN))


def table_data(table, x):
    high, low = halves(x)
    return mm(table[0], high, NT) + (mm(table[0], low, NT) + mm(table[1], high, NT))


def y_forward(read, emit, z, w_y, w_0, turn, groups, rows, lanes):
    def chunk(i, carry):
        out = rfft([read(i, a) for a in range(groups)])
        here = pl.ds(pl.multiple_of(i * SUB, SUB), SUB)
        z[0, here, :lanes] = out[0][0]
        z[0, here, lanes:] = out[groups // 2][0]
        for t in range(1, groups // 2):
            re, im = out[t]
            c, s = turn[t, 0:1, :], turn[t, 1:2, :]
            z[t, here, :lanes] = re * c - im * s
            z[t, here, lanes:] = re * s + im * c
        return carry

    lax.fori_loop(0, rows // SUB, chunk, 0)
    for t in range(groups // 2):
        emit(t, table_data(w_0 if t == 0 else w_y, z[t]))


def y_inverse(fetch, write, z, w_y, w_0, turn, groups, rows, lanes):
    for t in range(groups // 2):
        z[t] = data_table(fetch(t).T, w_0 if t == 0 else w_y)

    def chunk(i, carry):
        here = pl.ds(pl.multiple_of(i * SUB, SUB), SUB)
        zs = [(z[0, here, :lanes] * 2.0, None)]
        for t in range(1, groups // 2):
            re, im = z[t, here, :lanes], z[t, here, lanes:]
            c, s = turn[t, 0:1, :], turn[t, 1:2, :]
            zs.append((re * c + im * s, im * c - re * s))
        zs.append((z[0, here, lanes:] * 2.0, None))
        write(i, here, c2r(zs))
        return carry

    lax.fori_loop(0, rows // SUB, chunk, 0)


def x_radix(tile, z, base, turn, lanes, step):
    for t, (re, im) in enumerate(cfft(tile, -1.0)):
        here = pl.ds(pl.multiple_of(base + t * step, SUB), SUB)
        if t == 0:
            z[here, :lanes] = re
            z[here, lanes:] = im
        else:
            c, s = turn[t, 0:1, :], turn[t, 1:2, :]
            z[here, :lanes] = re * c - im * s
            z[here, lanes:] = re * s + im * c


def x_unradix(z, base, turn, groups, lanes, step):
    zs = []
    for t in range(groups):
        here = pl.ds(pl.multiple_of(base + t * step, SUB), SUB)
        re, im = z[here, :lanes], z[here, lanes:]
        if t:
            c, s = turn[t, 0:1, :], turn[t, 1:2, :]
            re, im = re * c + im * s, im * c - re * s
        zs.append((re, im))
    return cfft(zs, 1.0)


def fast_shards(volume, psf_spectra, background, measured):
    groups = lax.axis_size("row")
    depth, rows, length = volume.shape
    lanes = LANES
    tiles = groups // 2
    kept = tiles * SUB
    pair = 2 * SUB
    f32 = jnp.float32
    place = lax.axis_index("row")
    part = lax.axis_index("vol")
    w_y, w_0, w_x, w_xi, turn = (jnp.asarray(t) for t in make_tables(groups, lanes))
    own_rows = kept_rows(groups, rows)

    whole = lambda *shape: pl.BlockSpec(shape, lambda *_: (0,) * len(shape))
    y_specs = [whole(*w_y.shape), whole(*w_0.shape), whole(*turn.shape)]
    x_specs = [whole(*w_x.shape), whole(*w_xi.shape), whole(*turn.shape)]
    y_scratch = pltpu.VMEM((tiles, rows, 2 * lanes), f32)
    send_shape = (groups, tiles, 2, SUB, lanes)

    def many(n):
        return (groups, n, tiles, 2, SUB, lanes)

    low = place < groups // 2
    mid = rows // 2
    pick_send = np.zeros((kept, rows), np.float32)
    pick_own = np.zeros((kept, rows), np.float32)
    for r, k in enumerate(own_rows):
        pick_send[r, (rows - k) if k else mid] = 1.0
        pick_own[r, k] = 1.0
    pick_high = pick_own.copy()
    pick_high[0] = 0.0
    pick_high[0, mid] = 1.0

    def pick_kernel(part_ref, sel_ref, psf_ref, send_ref):
        send_ref[...] = mm(sel_ref[...], psf_ref[0, 0], NN)

    flags = jnp.stack([low.astype(jnp.int32), part.astype(jnp.int32), (place == 0).astype(jnp.int32)])
    smem = pl.BlockSpec(memory_space=pltpu.SMEM)
    bf = jnp.bfloat16
    sel_send = jnp.asarray(pick_send, bf)
    flip = [(p, groups - 1 - p) for p in range(groups)]
    sends, mine, other = [], [], []
    for d in range(depth):
        send = pl.pallas_call(
            pick_kernel,
            grid_spec=pltpu.PrefetchScalarGridSpec(
                num_scalar_prefetch=1,
                grid=(1,),
                in_specs=[whole(kept, rows),
                          pl.BlockSpec((1, 1, rows, length), lambda i, where, d=d: (where[1], d, 0, 0))],
                out_specs=whole(kept, length),
            ),
            out_shape=jax.ShapeDtypeStruct((kept, length), f32),
            name="pick",
        )(flags, sel_send, psf_spectra)
        sends.append(send)
    edge = psf_spectra[:, :, 0, :].astype(f32).reshape(2 * depth, length)
    edge = jnp.pad(edge, ((0, pair - 2 * depth), (0, 0)))
    edge, early, *sends = lax.optimization_barrier((edge, volume, *sends))
    ends = [(groups - p, p) for p in range(1, groups // 2)] + [(groups // 2, 0)]
    edge = lax.ppermute(edge, "row", ends)
    for d in range(depth):
        mine.append(lax.ppermute(sends[d], "row", flip))
    for d in range(depth):
        other.append(lax.ppermute(mine[d], "vol", [(0, 1), (1, 0)]))

    scale = 0.5 / (length * length)
    many_t = 2
    width = many_t * lanes

    def mix_kernel(where_ref, own_l_ref, own_h_ref, psf_ref, edge_ref, *rest):
        mine_refs, other_refs = rest[:depth], rest[depth:2 * depth]
        a_ref, b_ref, o_s, p_s, e_s = rest[2 * depth:]
        step = pl.program_id(0)

        @pl.when(step == 0)
        def _():
            zero = where_ref[2] == 1
            is_low = where_ref[0] == 1
            sel = jnp.where(is_low, own_l_ref[...], own_h_ref[...]).astype(bf)
            first = lax.broadcasted_iota(jnp.int32, (SUB, length), 0) == 0
            for c in range(2):
                mine_here = where_ref[1] == c
                for d in range(depth):
                    row = c * depth + d
                    base = row * kept
                    kept_own = mm(sel, psf_ref[c, d], NN)
                    o_s[base:base + kept, :] = kept_own.astype(bf)
                    p = jnp.where(mine_here, mine_refs[d][...], other_refs[d][...])
                    swap = jnp.where(zero, kept_own[0:1, :], edge_ref[row:row + 1, :])
                    head = jnp.where(jnp.logical_and(first, is_low), swap, p[:SUB])
                    p_s[base:base + kept, :] = jnp.concatenate([head, p[SUB:]], 0).astype(bf)
            e_s[...] = edge_ref[...].astype(bf)

        freq = lax.broadcasted_iota(jnp.int32, (length, width), 0)
        col = lax.broadcasted_iota(jnp.int32, (length, width), 1)
        target = (col % lanes) * groups + step * many_t + col // lanes
        hot = jnp.where(freq == target, 1.0, 0.0).astype(bf)
        hot_rev = jnp.where(freq == (length - target) % length, 1.0, 0.0).astype(bf)
        plain = mm(o_s[...], hot, NN)
        mirror = mm(p_s[...], hot_rev, NN)
        e_plain = mm(e_s[...], hot, NN)
        e_mirror = mm(e_s[...], hot_rev, NN)
        zero = jnp.where(where_ref[2] == 1, 1.0, 0.0).astype(f32)
        first = lax.broadcasted_iota(jnp.int32, (SUB, width), 0) == 0
        for c in range(2):
            sign = 1.0 if c == 0 else -1.0
            for d in range(depth):
                row = c * depth + d
                base = row * kept
                h = (plain[base:base + kept] + sign * mirror[base:base + kept]) * scale
                e = (e_plain[row:row + 1] + sign * e_mirror[row:row + 1]) * scale
                a0 = h[:SUB] * (1.0 - 0.75 * zero) + (0.25 * zero) * e
                b0 = (h[:SUB] - e) * (0.25 * zero)
                a_ref[c, d, :SUB, :] = jnp.where(first, a0, h[:SUB])
                a_ref[c, d, SUB:, :] = h[SUB:]
                b_ref[c, d, :SUB, :] = jnp.where(first, b0, 0.0)
                b_ref[c, d, SUB:, :] = jnp.zeros((SUB, width), f32)

    planes = 2 * depth * kept
    a_all, b_all = pl.pallas_call(
        mix_kernel,
        grid=(groups // many_t,),
        in_specs=[smem, whole(kept, rows), whole(kept, rows), whole(2, depth, rows, length),
                  whole(pair, length)] + [whole(kept, length)] * (2 * depth),
        out_specs=[pl.BlockSpec((2, depth, kept, width), lambda i: (0, 0, 0, i)),
                   pl.BlockSpec((2, depth, pair, width), lambda i: (0, 0, 0, i))],
        out_shape=[jax.ShapeDtypeStruct((2, depth, kept, length), f32),
                   jax.ShapeDtypeStruct((2, depth, pair, length), f32)],
        scratch_shapes=[pltpu.VMEM((planes, length), bf), pltpu.VMEM((planes, length), bf),
                        pltpu.VMEM((pair, length), bf)],
        name="mix",
    )(flags, jnp.asarray(pick_own), jnp.asarray(pick_high), psf_spectra, edge, *mine, *other)

    def forward_kernel(wy_ref, w0_ref, turn_ref, v_ref, o_ref, z):
        def read(i, a):
            return v_ref[0, pl.ds(pl.multiple_of(i * SUB, SUB), SUB), a * lanes:(a + 1) * lanes]

        def emit(t, out):
            o_ref[:, 0, t] = out.reshape(groups, 2, SUB, rows)

        y_forward(read, emit, z, wy_ref, w0_ref, turn_ref, groups, rows, lanes)

    outgoing = pl.pallas_call(
        forward_kernel,
        grid=(depth,),
        in_specs=y_specs + [pl.BlockSpec((1, rows, length), lambda d: (d, 0, 0))],
        out_specs=pl.BlockSpec((groups, 1, tiles, 2, SUB, lanes), lambda d: (0, d, 0, 0, 0, 0)),
        out_shape=jax.ShapeDtypeStruct(many(depth), f32),
        scratch_shapes=[y_scratch],
        name="forward_y",
    )(w_y, w_0, turn, early)

    def swap(field):
        return lax.all_to_all(field, "row", split_axis=0, concat_axis=0, tiled=True)

    outgoing, _ = lax.optimization_barrier((outgoing, mine[depth // 2]))
    arrived = swap(outgoing)

    block = groups * pair
    x_scratch = lambda n: pltpu.VMEM((n * block, 2 * lanes), f32)

    def source(s_ref, d, h, flipped=False):
        out = []
        for s in range(groups):
            re, im = s_ref[s, d, h, 0], s_ref[s, d, h, 1]
            out.append((re, -im if flipped else im))
        return out

    def project_kernel(wx_ref, wxi_ref, turn_ref, s_ref, a_ref, b_ref, o_ref, z, t_s, zc):
        def gather(flipped):
            def one(i, carry):
                d, h = i // 2, i % 2
                x_radix(source(s_ref, d, h, flipped), z, d * block + h * SUB, turn_ref, lanes, pair)
                return carry

            lax.fori_loop(0, 2 * depth, one, 0)
            for d in range(depth):
                zc[d * block:(d + 1) * block, :] = data_table(z[d * block:(d + 1) * block, :], wx_ref)

        def multiply(k_ref, fresh):
            for t in range(groups):
                here = slice(t * pair, (t + 1) * pair)
                cols = slice(t * lanes, (t + 1) * lanes)
                re, im = (None, None) if fresh else (t_s[here, :lanes], t_s[here, lanes:])
                for d in range(depth):
                    at = slice(d * block + t * pair, d * block + (t + 1) * pair)
                    zr, zi = zc[at, :lanes], zc[at, lanes:]
                    kr, ki = k_ref[0, d, :, cols], k_ref[1, d, :, cols]
                    re = plus(re, zr * kr - zi * ki)
                    im = plus(im, zr * ki + zi * kr)
                t_s[here, :lanes] = re
                t_s[here, lanes:] = im

        gather(False)
        multiply(a_ref, True)

        @pl.when(pl.program_id(0) == 0)
        def _():
            gather(True)
            multiply(b_ref, False)

        zc[:block, :] = data_table(t_s[...], wxi_ref)

        def back(h, carry):
            for s, (re, im) in enumerate(x_unradix(zc, h * SUB, turn_ref, groups, lanes, pair)):
                o_ref[s, h, 0] = re
                o_ref[s, h, 1] = im
            return carry

        lax.fori_loop(0, 2, back, 0)

    k_specs = [pl.BlockSpec((2, depth, pair, length), lambda j: (0, 0, j, 0)),
               whole(2, depth, pair, length)]
    one_spec = pl.BlockSpec((groups, 2, 2, SUB, lanes), lambda j: (0, j, 0, 0, 0))
    all_spec = pl.BlockSpec((groups, depth, 2, 2, SUB, lanes), lambda j: (0, 0, j, 0, 0, 0))
    outgoing = pl.pallas_call(
        project_kernel,
        grid=(tiles // 2,),
        in_specs=x_specs + [all_spec] + k_specs,
        out_specs=one_spec,
        out_shape=jax.ShapeDtypeStruct(send_shape, f32),
        scratch_shapes=[x_scratch(depth), x_scratch(1), x_scratch(depth)],
        name="project_x",
    )(w_x, w_xi, turn, arrived, a_all, b_all)
    arrived = swap(outgoing)

    def ratio_kernel(wy_ref, w0_ref, turn_ref, g_ref, bg_ref, me_ref, p_ref, o_ref, z, q_s):
        def fetch(t):
            return g_ref[:, t].reshape(groups * 2 * SUB, rows)

        def write(i, here, outs):
            for a, value in enumerate(outs):
                cols = slice(a * lanes, (a + 1) * lanes)
                p_ref[here, cols] = value
                q_s[here, cols] = me_ref[here, cols] / jnp.maximum(value + bg_ref[here, cols], FLOOR)

        y_inverse(fetch, write, z, wy_ref, w0_ref, turn_ref, groups, rows, lanes)

        def read(i, a):
            return q_s[pl.ds(pl.multiple_of(i * SUB, SUB), SUB), a * lanes:(a + 1) * lanes]

        def emit(t, out):
            o_ref[:, t] = out.reshape(groups, 2, SUB, rows)

        y_forward(read, emit, z, wy_ref, w0_ref, turn_ref, groups, rows, lanes)

    projection, outgoing = pl.pallas_call(
        ratio_kernel,
        out_shape=[jax.ShapeDtypeStruct((rows, length), f32), jax.ShapeDtypeStruct(send_shape, f32)],
        scratch_shapes=[y_scratch, pltpu.VMEM((rows, length), f32)],
        name="ratio",
    )(w_y, w_0, turn, arrived, background, measured)
    arrived = swap(outgoing)

    def correct_kernel(wx_ref, wxi_ref, turn_ref, s_ref, a_ref, b_ref, o_ref, z, zq, zc, c_s):
        def gather(flipped, out):
            def one(h, carry):
                tile = []
                for s in range(groups):
                    re, im = s_ref[s, h, 0], s_ref[s, h, 1]
                    tile.append((re, -im if flipped else im))
                x_radix(tile, z, h * SUB, turn_ref, lanes, pair)
                return carry

            lax.fori_loop(0, 2, one, 0)
            out[...] = data_table(z[...], wx_ref)

        def multiply(k_ref, src, fresh):
            for t in range(groups):
                here = slice(t * pair, (t + 1) * pair)
                cols = slice(t * lanes, (t + 1) * lanes)
                zr, zi = src[here, :lanes], src[here, lanes:]
                for d in range(depth):
                    at = slice(d * block + t * pair, d * block + (t + 1) * pair)
                    kr, ki = k_ref[0, d, :, cols], k_ref[1, d, :, cols]
                    re, im = zr * kr + zi * ki, zi * kr - zr * ki
                    if not fresh:
                        re, im = re + c_s[at, :lanes], im + c_s[at, lanes:]
                    c_s[at, :lanes] = re
                    c_s[at, lanes:] = im

        gather(False, zq)
        multiply(a_ref, zq, True)

        @pl.when(pl.program_id(0) == 0)
        def _():
            gather(True, zq)
            multiply(b_ref, zq, False)

        for d in range(depth):
            zc[d * block:(d + 1) * block, :] = data_table(c_s[d * block:(d + 1) * block, :], wxi_ref)

        def back(i, carry):
            d, h = i // 2, i % 2
            out = x_unradix(zc, d * block + h * SUB, turn_ref, groups, lanes, pair)
            for s, (re, im) in enumerate(out):
                o_ref[s, d, h, 0] = re
                o_ref[s, d, h, 1] = im
            return carry

        lax.fori_loop(0, 2 * depth, back, 0)

    outgoing = pl.pallas_call(
        correct_kernel,
        grid=(tiles // 2,),
        in_specs=x_specs + [one_spec] + k_specs,
        out_specs=all_spec,
        out_shape=jax.ShapeDtypeStruct(many(depth), f32),
        scratch_shapes=[x_scratch(1), x_scratch(1), x_scratch(depth), x_scratch(depth)],
        name="correct_x",
    )(w_x, w_xi, turn, arrived, a_all, b_all)
    arrived = swap(outgoing)

    def final_kernel(wy_ref, w0_ref, turn_ref, g_ref, v_ref, o_ref, z):
        def fetch(t):
            return g_ref[:, 0, t].reshape(groups * 2 * SUB, rows)

        def write(i, here, outs):
            for a, value in enumerate(outs):
                cols = slice(a * lanes, (a + 1) * lanes)
                o_ref[0, here, cols] = v_ref[0, here, cols] * value

        y_inverse(fetch, write, z, wy_ref, w0_ref, turn_ref, groups, rows, lanes)

    new_volume = pl.pallas_call(
        final_kernel,
        grid=(depth,),
        in_specs=y_specs + [
            pl.BlockSpec((groups, 1, tiles, 2, SUB, lanes), lambda d: (0, d, 0, 0, 0, 0)),
            pl.BlockSpec((1, rows, length), lambda d: (d, 0, 0))],
        out_specs=pl.BlockSpec((1, rows, length), lambda d: (d, 0, 0)),
        out_shape=jax.ShapeDtypeStruct((depth, rows, length), f32),
        scratch_shapes=[y_scratch],
        name="final_y",
    )(w_y, w_0, turn, arrived, volume)
    return new_volume, projection


def solution(mesh):
    groups, parts = mesh.shape["row"], mesh.shape["vol"]

    def shards(volume, psf_spectra, background, measured):
        rows = volume.shape[1]
        fits = parts == 2 and rows == LANES and rows == SUB * groups
        body = fast_shards if fits else generic_shards
        return body(volume, psf_spectra, background, measured)

    in_specs = (
        P("vol", "row", None),
        P(None, None, "row", None),
        P("row", None),
        P(("vol", "row"), None),
    )
    out_specs = (P("vol", "row", None), P(("vol", "row"), None))
    return jax.shard_map(shards, mesh=mesh, in_specs=in_specs, out_specs=out_specs, check_vma=False)
```

```python
import math

import jax
import jax.numpy as jnp
import numpy as np
from jax import lax
from jax.experimental import pallas as pl
from jax.experimental.pallas import tpu as pltpu
from jax.sharding import PartitionSpec as P


FLOOR = 0.5
HIGHEST = lax.Precision.HIGHEST
LANES = 128
SUB = 8


def phase_pair(first_extent, second_extent, modulus, direction):
    first_idx = jnp.arange(first_extent, dtype=jnp.int32)
    second_idx = jnp.arange(second_extent, dtype=jnp.int32)
    phases = first_idx[:, None] * second_idx[None, :] % modulus
    angles = phases.astype(jnp.float32) * (2.0 * math.pi / modulus)
    return (jnp.cos(angles), direction * jnp.sin(angles))


def contract(pattern, fields, coeffs, real_only):
    real_part, imag_part = fields
    coeff_real, coeff_imag = coeffs

    def product(operand, table_side):
        return jnp.einsum(pattern, operand, table_side, precision=HIGHEST)

    if imag_part is None:
        return (product(real_part, coeff_real), product(real_part, coeff_imag))
    out_real = product(real_part, coeff_real) - product(imag_part, coeff_imag)
    if real_only:
        return (out_real, None)
    return (out_real, product(real_part, coeff_imag) + product(imag_part, coeff_real))


def rotate(fields, factors):
    real_part, imag_part = fields
    factor_real, factor_imag = factors
    return (
        real_part * factor_real - imag_part * factor_imag,
        real_part * factor_imag + imag_part * factor_real,
    )


def leading_pass(fields, groups, direction):
    batch_size, row_count, length = fields[0].shape
    inner_count = length // groups
    shaped = tuple(
        None if member is None else member.reshape(batch_size, row_count, inner_count, groups)
        for member in fields
    )
    sectioned = contract(
        "bqnm,nk->bqkm", shaped, phase_pair(inner_count, inner_count, inner_count, direction), False
    )
    sectioned = rotate(sectioned, phase_pair(inner_count, groups, length, direction))
    sectioned = contract(
        "bqkm,mp->bpkq", sectioned, phase_pair(groups, groups, groups, direction), False
    )
    return tuple(member.reshape(batch_size, groups, inner_count * row_count) for member in sectioned)


def trailing_pass(fields, row_count, direction, real_only):
    batch_size, groups, merged = fields[0].shape
    inner_count = merged // row_count
    length = groups * row_count
    shaped = tuple(member.reshape(batch_size, groups, inner_count, row_count) for member in fields)
    sectioned = contract(
        "bskq,st->bktq", shaped, phase_pair(groups, groups, groups, direction), False
    )
    sectioned = rotate(sectioned, phase_pair(groups, row_count, length, direction))
    sectioned = contract(
        "bktq,qu->bkut", sectioned, phase_pair(row_count, row_count, row_count, direction), real_only
    )
    return tuple(
        None if member is None else member.reshape(batch_size, inner_count, length)
        for member in sectioned
    )


def generic_shards(volume, psf_spectra, background, measured):
    groups = lax.axis_size("row")
    row_count = volume.shape[1]
    length = volume.shape[2]
    inverse_scale = 1.0 / (length * length)
    response_real = psf_spectra[0].astype(jnp.float32)
    response_imag = psf_spectra[1].astype(jnp.float32)

    def swap(field):
        return lax.all_to_all(field, "row", split_axis=1, concat_axis=1, tiled=True)

    outgoing = leading_pass((volume, None), groups, -1.0)
    spec_real, spec_imag = trailing_pass(
        (swap(outgoing[0]), swap(outgoing[1])), row_count, -1.0, False
    )
    prod_real = spec_real * response_real - spec_imag * response_imag
    prod_imag = spec_real * response_imag + spec_imag * response_real
    summed = (jnp.sum(prod_real, axis=0, keepdims=True), jnp.sum(prod_imag, axis=0, keepdims=True))
    outgoing = leading_pass(summed, groups, 1.0)
    arrived = (swap(outgoing[0]), swap(outgoing[1]))
    projection = trailing_pass(arrived, row_count, 1.0, True)[0][0] * inverse_scale
    quotient = measured / jnp.maximum(projection + background, FLOOR)
    outgoing = leading_pass((quotient[None], None), groups, -1.0)
    arrived = (swap(outgoing[0]), swap(outgoing[1]))
    ratio_real, ratio_imag = trailing_pass(arrived, row_count, -1.0, False)
    corr_real = ratio_real * response_real + ratio_imag * response_imag
    corr_imag = ratio_imag * response_real - ratio_real * response_imag
    outgoing = leading_pass((corr_real, corr_imag), groups, 1.0)
    arrived = (swap(outgoing[0]), swap(outgoing[1]))
    correction = trailing_pass(arrived, row_count, 1.0, True)[0] * inverse_scale
    return (volume * correction, projection)


def times(z, angle):
    re, im = z
    c, s = math.cos(angle), math.sin(angle)
    if abs(s) < 1e-12:
        return z if c > 0 else (-re, None if im is None else -im)
    if abs(c) < 1e-12:
        if im is None:
            return (None, re if s > 0 else -re)
        return (-im, re) if s > 0 else (im, -re)
    if im is None:
        return (re * c, re * s)
    if abs(abs(c) - abs(s)) < 1e-12:
        sc, ss = math.copysign(1.0, c), math.copysign(1.0, s)
        a = re if sc > 0 else -re
        b = im if sc > 0 else -im
        r, i = (a - im, b + re) if ss > 0 else (a + im, b - re)
        return (r * abs(c), i * abs(c))
    return (re * c - im * s, re * s + im * c)


def plus(a, b):
    if a is None:
        return b
    return a if b is None else a + b


def minus(a, b):
    if b is None:
        return a
    return -b if a is None else a - b


def cadd(a, b):
    return (plus(a[0], b[0]), plus(a[1], b[1]))


def csub(a, b):
    return (minus(a[0], b[0]), minus(a[1], b[1]))


def conj(a):
    return (a[0], None if a[1] is None else -a[1])


def cfft(xs, sign):
    n = len(xs)
    if n == 1:
        return list(xs)
    even, odd = cfft(xs[0::2], sign), cfft(xs[1::2], sign)
    turned = [times(odd[t], sign * 2.0 * math.pi * t / n) for t in range(n // 2)]
    return [cadd(even[t], turned[t]) for t in range(n // 2)] + [
        csub(even[t], turned[t]) for t in range(n // 2)
    ]


def rfft(xs):
    n = len(xs)
    if n == 2:
        return [(xs[0] + xs[1], None), (xs[0] - xs[1], None)]
    even, odd = rfft(xs[0::2]), rfft(xs[1::2])
    out = [None] * (n // 2 + 1)
    for t in range(n // 4 + 1):
        turned = times(odd[t], -2.0 * math.pi * t / n)
        out[t] = cadd(even[t], turned)
        if t < n // 4:
            out[n // 2 - t] = conj(csub(even[t], turned))
    return out


def c2r(zs):
    n = 2 * (len(zs) - 1)
    if n == 2:
        return [zs[0][0] + zs[1][0], zs[0][0] - zs[1][0]]
    q = n // 4
    even, odd = [], []
    for t in range(q):
        mirror = conj(zs[n // 2 - t])
        even.append(cadd(zs[t], mirror))
        odd.append(times(csub(zs[t], mirror), 2.0 * math.pi * t / n))
    even.append((zs[q][0] * 2.0, None))
    odd.append((zs[q][1] * -2.0, None))
    a, b = c2r(even), c2r(odd)
    return [half[i] for i in range(n // 2) for half in (a, b)]


def split_table(table):
    high = table.astype(jnp.bfloat16)
    low = (table - high.astype(np.float64)).astype(jnp.bfloat16)
    return np.stack([high, low])


def make_tables(groups, lanes):
    length = groups * lanes
    per = lanes // groups
    pos = np.arange(lanes)
    w_y = np.zeros((groups, 2, SUB, 2, lanes))
    w_0 = np.zeros((groups, 2, SUB, 2, lanes))
    half = SUB // 2
    for p in range(groups):
        for r in range(SUB):
            ang = 2.0 * np.pi * ((per * p + r) * pos % lanes) / lanes
            w_y[p, 0, r] = np.cos(ang), np.sin(ang)
            w_y[p, 1, r] = -np.sin(ang), np.cos(ang)
            if r < half:
                unit = per * p + r
                if r == 0 and p >= groups // 2:
                    unit = per * p + per // 2
                ang = 2.0 * np.pi * (groups * unit * pos % length) / length
                w_0[p, 0, r, 0] = np.cos(ang)
                w_0[p, 1, r, 0] = -np.sin(ang)
                if r == 0 and p == 0:
                    w_0[p, 1, r, 0] = (-1.0) ** pos
            else:
                ang = (groups * (per * p + r - half) + groups // 2) * pos % length
                ang = 2.0 * np.pi * ang / length
                w_0[p, 0, r, 1] = np.cos(ang)
                w_0[p, 1, r, 1] = -np.sin(ang)
    rows = groups * 2 * SUB
    ang = 2.0 * np.pi * (pos[:, None] * pos[None, :] % lanes) / lanes
    w_x = np.block([[np.cos(ang), -np.sin(ang)], [np.sin(ang), np.cos(ang)]])
    ang = 2.0 * np.pi * (np.arange(groups)[:, None] * pos[None, :] % length) / length
    turn = np.stack([np.cos(ang), -np.sin(ang)], axis=1).astype(np.float32)
    return (
        split_table(w_y.reshape(rows, 2 * lanes)),
        split_table(w_0.reshape(rows, 2 * lanes)),
        split_table(w_x),
        split_table(w_x.T),
        turn,
    )


def kept_rows(groups, lanes):
    per = lanes // groups
    half = SUB // 2
    own = [groups * w for w in range(half)] + [groups * w + groups // 2 for w in range(half)]
    for tile in range(1, groups // 2):
        own += [groups * w + tile for w in range(per)]
    return own


NN = (((1,), (0,)), ((), ()))
NT = (((1,), (1,)), ((), ()))


def halves(x):
    high = x.astype(jnp.bfloat16)
    return high, (x - high.astype(jnp.float32)).astype(jnp.bfloat16)


def mm(a, b, dims):
    return lax.dot_general(a, b, dims, preferred_element_type=jnp.float32)


def data_table(x, table):
    high, low = halves(x)
    return mm(high, table[0], NN) + (mm(low, table[0], NN) + mm(high, table[1], NN))


def table_data(table, x):
    high, low = halves(x)
    return mm(table[0], high, NT) + (mm(table[0], low, NT) + mm(table[1], high, NT))


def y_forward(read, emit, z, w_y, w_0, turn, groups, rows, lanes):
    def chunk(i, carry):
        out = rfft([read(i, a) for a in range(groups)])
        here = pl.ds(pl.multiple_of(i * SUB, SUB), SUB)
        z[0, here, :lanes] = out[0][0]
        z[0, here, lanes:] = out[groups // 2][0]
        for t in range(1, groups // 2):
            re, im = out[t]
            c, s = turn[t, 0:1, :], turn[t, 1:2, :]
            z[t, here, :lanes] = re * c - im * s
            z[t, here, lanes:] = re * s + im * c
        return carry

    lax.fori_loop(0, rows // SUB, chunk, 0)
    for t in range(groups // 2):
        emit(t, table_data(w_0 if t == 0 else w_y, z[t]))


def y_inverse(fetch, write, z, w_y, w_0, turn, groups, rows, lanes):
    for t in range(groups // 2):
        z[t] = data_table(fetch(t).T, w_0 if t == 0 else w_y)

    def chunk(i, carry):
        here = pl.ds(pl.multiple_of(i * SUB, SUB), SUB)
        zs = [(z[0, here, :lanes] * 2.0, None)]
        for t in range(1, groups // 2):
            re, im = z[t, here, :lanes], z[t, here, lanes:]
            c, s = turn[t, 0:1, :], turn[t, 1:2, :]
            zs.append((re * c + im * s, im * c - re * s))
        zs.append((z[0, here, lanes:] * 2.0, None))
        write(i, here, c2r(zs))
        return carry

    lax.fori_loop(0, rows // SUB, chunk, 0)


def x_radix(tile, z, base, turn, lanes, step):
    for t, (re, im) in enumerate(cfft(tile, -1.0)):
        here = pl.ds(pl.multiple_of(base + t * step, SUB), SUB)
        if t == 0:
            z[here, :lanes] = re
            z[here, lanes:] = im
        else:
            c, s = turn[t, 0:1, :], turn[t, 1:2, :]
            z[here, :lanes] = re * c - im * s
            z[here, lanes:] = re * s + im * c


def x_unradix(z, base, turn, groups, lanes, step):
    zs = []
    for t in range(groups):
        here = pl.ds(pl.multiple_of(base + t * step, SUB), SUB)
        re, im = z[here, :lanes], z[here, lanes:]
        if t:
            c, s = turn[t, 0:1, :], turn[t, 1:2, :]
            re, im = re * c + im * s, im * c - re * s
        zs.append((re, im))
    return cfft(zs, 1.0)


def fast_shards(volume, psf_spectra, background, measured):
    groups = lax.axis_size("row")
    depth, rows, length = volume.shape
    lanes = LANES
    tiles = groups // 2
    kept = tiles * SUB
    pair = 2 * SUB
    f32 = jnp.float32
    place = lax.axis_index("row")
    part = lax.axis_index("vol")
    w_y, w_0, w_x, w_xi, turn = (jnp.asarray(t) for t in make_tables(groups, lanes))
    own_rows = kept_rows(groups, rows)

    whole = lambda *shape: pl.BlockSpec(shape, lambda *_: (0,) * len(shape))
    near = pl.BlockSpec(memory_space=pltpu.VMEM)

    def keep(x):
        return pltpu.with_memory_space_constraint(x, pltpu.VMEM)

    def far(x):
        return pltpu.with_memory_space_constraint(x, pltpu.HBM)

    y_tables, x_tables = (w_y, w_0, turn), (w_x, w_xi, turn)
    y_near = tuple(keep(t) for t in y_tables)
    x_near = tuple(keep(t) for t in x_tables)
    y_specs = [whole(*t.shape) for t in y_tables]
    x_specs = [whole(*t.shape) for t in x_tables]
    y_scratch = pltpu.VMEM((tiles, rows, 2 * lanes), f32)
    send_shape = (groups, tiles, 2, SUB, lanes)

    def many(n):
        return (groups, n, tiles, 2, SUB, lanes)

    low = place < groups // 2
    mid = rows // 2
    pick_send = np.zeros((kept, rows), np.float32)
    pick_own = np.zeros((kept, rows), np.float32)
    for r, k in enumerate(own_rows):
        pick_send[r, (rows - k) if k else mid] = 1.0
        pick_own[r, k] = 1.0
    pick_high = pick_own.copy()
    pick_high[0] = 0.0
    pick_high[0, mid] = 1.0

    def pick_kernel(part_ref, sel_ref, psf_ref, send_ref):
        send_ref[...] = mm(sel_ref[...], psf_ref[0, 0], NN)

    flags = jnp.stack([low.astype(jnp.int32), part.astype(jnp.int32), (place == 0).astype(jnp.int32)])
    smem = pl.BlockSpec(memory_space=pltpu.SMEM)
    bf = jnp.bfloat16
    sel_send = jnp.asarray(pick_send, bf)
    flip = [(p, groups - 1 - p) for p in range(groups)]
    sends, mine, other = [], [], []
    for d in range(depth):
        send = pl.pallas_call(
            pick_kernel,
            grid_spec=pltpu.PrefetchScalarGridSpec(
                num_scalar_prefetch=1,
                grid=(1,),
                in_specs=[whole(kept, rows),
                          pl.BlockSpec((1, 1, rows, length), lambda i, where, d=d: (where[0], d, 0, 0))],
                out_specs=whole(kept, length),
            ),
            out_shape=jax.ShapeDtypeStruct((kept, length), f32),
            name="pick",
        )(part.astype(jnp.int32).reshape(1), sel_send, psf_spectra)
        sends.append(send)
        mine.append(lax.ppermute(send, "row", flip))
    late, early, _ = lax.optimization_barrier((psf_spectra, volume, sends[-1]))
    edge = late[:, :, 0, :].astype(f32).reshape(2 * depth, length)
    edge = jnp.pad(edge, ((0, pair - 2 * depth), (0, 0)))
    ends = [(groups - p, p) for p in range(1, groups // 2)] + [(groups // 2, 0)]
    edge = lax.ppermute(edge, "row", ends)
    for d in range(depth):
        other.append(lax.ppermute(mine[d], "vol", [(0, 1), (1, 0)]))

    scale = 0.5 / (length * length)
    many_t = 2
    width = many_t * lanes

    def mix_kernel(where_ref, own_l_ref, own_h_ref, psf_ref, edge_ref, *rest):
        mine_refs, other_refs = rest[:depth], rest[depth:2 * depth]
        a_ref, b_ref, o_s, p_s, e_s = rest[2 * depth:]
        step = pl.program_id(0)

        @pl.when(step == 0)
        def _():
            zero = where_ref[2] == 1
            is_low = where_ref[0] == 1
            sel = jnp.where(is_low, own_l_ref[...], own_h_ref[...]).astype(bf)
            first = lax.broadcasted_iota(jnp.int32, (SUB, length), 0) == 0
            for c in range(2):
                mine_here = where_ref[1] == c
                for d in range(depth):
                    row = c * depth + d
                    base = row * kept
                    kept_own = mm(sel, psf_ref[c, d], NN)
                    o_s[base:base + kept, :] = kept_own.astype(bf)
                    p = jnp.where(mine_here, mine_refs[d][...], other_refs[d][...])
                    swap = jnp.where(zero, kept_own[0:1, :], edge_ref[row:row + 1, :])
                    head = jnp.where(jnp.logical_and(first, is_low), swap, p[:SUB])
                    p_s[base:base + kept, :] = jnp.concatenate([head, p[SUB:]], 0).astype(bf)
            e_s[...] = edge_ref[...].astype(bf)

        freq = lax.broadcasted_iota(jnp.int32, (length, width), 0)
        col = lax.broadcasted_iota(jnp.int32, (length, width), 1)
        target = (col % lanes) * groups + step * many_t + col // lanes
        hot = jnp.where(freq == target, 1.0, 0.0).astype(bf)
        hot_rev = jnp.where(freq == (length - target) % length, 1.0, 0.0).astype(bf)
        plain = mm(o_s[...], hot, NN)
        mirror = mm(p_s[...], hot_rev, NN)
        e_plain = mm(e_s[...], hot, NN)
        e_mirror = mm(e_s[...], hot_rev, NN)
        zero = jnp.where(where_ref[2] == 1, 1.0, 0.0).astype(f32)
        b_ref[...] = jnp.zeros((2, SUB, width), f32)
        first = lax.broadcasted_iota(jnp.int32, (SUB, width), 0) == 0
        for c in range(2):
            sign = 1.0 if c == 0 else -1.0
            for d in range(depth):
                row = c * depth + d
                base = row * kept
                h = (plain[base:base + kept] + sign * mirror[base:base + kept]) * scale
                e = (e_plain[row:row + 1] + sign * e_mirror[row:row + 1]) * scale
                a0 = h[:SUB] * (1.0 - 0.75 * zero) + (0.25 * zero) * e
                b0 = (h[:SUB] - e) * (0.25 * zero)
                a_ref[c, d, :SUB, :] = jnp.where(first, a0, h[:SUB])
                a_ref[c, d, SUB:, :] = h[SUB:]
                b_ref[c, d:d + 1, :] = b0[0:1, :]

    planes = 2 * depth * kept
    a_all, b_all = pl.pallas_call(
        mix_kernel,
        grid=(groups // many_t,),
        in_specs=[smem, whole(kept, rows), whole(kept, rows), whole(2, depth, rows, length),
                  whole(pair, length)] + [whole(kept, length)] * (2 * depth),
        out_specs=[pl.BlockSpec((2, depth, kept, width), lambda i: (0, 0, 0, i)),
                   pl.BlockSpec((2, SUB, width), lambda i: (0, 0, i))],
        out_shape=[jax.ShapeDtypeStruct((2, depth, kept, length), f32),
                   jax.ShapeDtypeStruct((2, SUB, length), f32)],
        scratch_shapes=[pltpu.VMEM((planes, length), bf), pltpu.VMEM((planes, length), bf),
                        pltpu.VMEM((pair, length), bf)],
        name="mix",
    )(flags, jnp.asarray(pick_own), jnp.asarray(pick_high), psf_spectra, edge, *mine, *other)

    def forward_kernel(wy_ref, w0_ref, turn_ref, v_ref, o_ref, z):
        def read(i, a):
            return v_ref[0, pl.ds(pl.multiple_of(i * SUB, SUB), SUB), a * lanes:(a + 1) * lanes]

        def emit(t, out):
            o_ref[:, 0, t] = out.reshape(groups, 2, SUB, rows)

        y_forward(read, emit, z, wy_ref, w0_ref, turn_ref, groups, rows, lanes)

    outgoing = pl.pallas_call(
        forward_kernel,
        grid=(depth,),
        in_specs=y_specs + [pl.BlockSpec((1, rows, length), lambda d: (d, 0, 0))],
        out_specs=pl.BlockSpec((groups, 1, tiles, 2, SUB, lanes), lambda d: (0, d, 0, 0, 0, 0)),
        out_shape=jax.ShapeDtypeStruct(many(depth), f32),
        scratch_shapes=[y_scratch],
        name="forward_y",
    )(*y_tables, early)

    def swap(field):
        return lax.all_to_all(field, "row", split_axis=0, concat_axis=0, tiled=True)

    outgoing, _ = lax.optimization_barrier((outgoing, mine[0]))
    arrived = swap(outgoing)

    block = groups * pair
    x_scratch = lambda n: pltpu.VMEM((n * block, 2 * lanes), f32)

    small = groups * SUB
    lead = lambda: lax.broadcasted_iota(jnp.int32, (SUB, lanes), 0)

    def project_kernel(wx_ref, wxi_ref, turn_ref, s_ref, a_ref, b_ref, o_ref, z, t_s, zc):
        def one(i, carry):
            d, h = i // 2, i % 2
            j = pl.program_id(0) * 2 + h
            tile = [(s_ref[s, d, j, 0], s_ref[s, d, j, 1]) for s in range(groups)]
            x_radix(tile, z, d * block + h * SUB, turn_ref, lanes, pair)
            return carry

        lax.fori_loop(0, 2 * depth, one, 0)
        for d in range(depth):
            zc[d * block:(d + 1) * block, :] = data_table(z[d * block:(d + 1) * block, :], wx_ref)
        for t in range(groups):
            here = slice(t * pair, (t + 1) * pair)
            cols = slice(t * lanes, (t + 1) * lanes)
            re = im = None
            for d in range(depth):
                at = slice(d * block + t * pair, d * block + (t + 1) * pair)
                zr, zi = zc[at, :lanes], zc[at, lanes:]
                kr, ki = a_ref[0, d, :, cols], a_ref[1, d, :, cols]
                re = plus(re, zr * kr - zi * ki)
                im = plus(im, zr * ki + zi * kr)
            t_s[here, :lanes] = re
            t_s[here, lanes:] = im

        @pl.when(pl.program_id(0) == 0)
        def _():
            def row(s, c):
                out = s_ref[s, 0, 0, c, 0:1, :]
                for d in range(1, depth):
                    out = jnp.where(lead() == d, s_ref[s, d, 0, c, 0:1, :], out)
                return jnp.broadcast_to(out, (SUB, lanes))

            x_radix([(row(s, 0), -row(s, 1)) for s in range(groups)], z, 0, turn_ref, lanes, SUB)
            zc[:small, :] = data_table(z[:small, :], wx_ref)
            for t in range(groups):
                at = slice(t * SUB, (t + 1) * SUB)
                cols = slice(t * lanes, (t + 1) * lanes)
                zr, zi = zc[at, :lanes], zc[at, lanes:]
                kr, ki = b_ref[0, :, cols], b_ref[1, :, cols]
                top = slice(t * pair, t * pair + 1)
                t_s[top, :lanes] += jnp.sum(zr * kr - zi * ki, axis=0, keepdims=True)
                t_s[top, lanes:] += jnp.sum(zr * ki + zi * kr, axis=0, keepdims=True)

        zc[:block, :] = data_table(t_s[...], wxi_ref)

        def back(h, carry):
            j = pl.program_id(0) * 2 + h
            for s, (re, im) in enumerate(x_unradix(zc, h * SUB, turn_ref, groups, lanes, pair)):
                o_ref[s, j, 0] = re
                o_ref[s, j, 1] = im
            return carry

        lax.fori_loop(0, 2, back, 0)

    k_specs = [pl.BlockSpec((2, depth, pair, length), lambda j: (0, 0, j, 0)), whole(2, SUB, length)]
    outgoing = pl.pallas_call(
        project_kernel,
        grid=(tiles // 2,),
        in_specs=x_specs + [near] + k_specs,
        out_specs=near,
        out_shape=pltpu.VMEM(send_shape, f32),
        scratch_shapes=[x_scratch(depth), x_scratch(1), x_scratch(depth)],
        compiler_params=pltpu.CompilerParams(vmem_limit_bytes=24 << 20),
        name="project_x",
    )(*(far(t) for t in x_tables), keep(arrived), far(a_all), far(b_all))
    arrived = swap(outgoing)

    def ratio_kernel(wy_ref, w0_ref, turn_ref, g_ref, bg_ref, me_ref, p_ref, o_ref, z, q_s):
        def fetch(t):
            return g_ref[:, t].reshape(groups * 2 * SUB, rows)

        def write(i, here, outs):
            for a, value in enumerate(outs):
                cols = slice(a * lanes, (a + 1) * lanes)
                p_ref[here, cols] = value
                q_s[here, cols] = me_ref[here, cols] / jnp.maximum(value + bg_ref[here, cols], FLOOR)

        y_inverse(fetch, write, z, wy_ref, w0_ref, turn_ref, groups, rows, lanes)

        def read(i, a):
            return q_s[pl.ds(pl.multiple_of(i * SUB, SUB), SUB), a * lanes:(a + 1) * lanes]

        def emit(t, out):
            o_ref[:, t] = out.reshape(groups, 2, SUB, rows)

        y_forward(read, emit, z, wy_ref, w0_ref, turn_ref, groups, rows, lanes)

    projection, outgoing = pl.pallas_call(
        ratio_kernel,
        in_specs=[near] * 3 + [near] * 3,
        out_specs=[whole(rows, length), near],
        out_shape=[jax.ShapeDtypeStruct((rows, length), f32), pltpu.VMEM(send_shape, f32)],
        scratch_shapes=[y_scratch, pltpu.VMEM((rows, length), f32)],
        compiler_params=pltpu.CompilerParams(vmem_limit_bytes=16 << 20),
        name="ratio",
    )(*y_near, keep(arrived), keep(background), keep(measured))
    arrived = swap(outgoing)

    def correct_kernel(wx_ref, wxi_ref, turn_ref, s_ref, a_ref, b_ref, o_ref, z, zq, zc, c_s):
        mine_rows = pl.ds(pl.multiple_of(pl.program_id(0) * pair, pair), pair)

        def one(h, carry):
            j = pl.program_id(0) * 2 + h
            tile = [(s_ref[s, j, 0], s_ref[s, j, 1]) for s in range(groups)]
            x_radix(tile, z, h * SUB, turn_ref, lanes, pair)
            return carry

        lax.fori_loop(0, 2, one, 0)
        zq[...] = data_table(z[...], wx_ref)
        for t in range(groups):
            here = slice(t * pair, (t + 1) * pair)
            cols = slice(t * lanes, (t + 1) * lanes)
            zr, zi = zq[here, :lanes], zq[here, lanes:]
            for d in range(depth):
                at = slice(d * block + t * pair, d * block + (t + 1) * pair)
                kr, ki = a_ref[0, d, mine_rows, cols], a_ref[1, d, mine_rows, cols]
                c_s[at, :lanes] = zr * kr + zi * ki
                c_s[at, lanes:] = zi * kr - zr * ki

        @pl.when(pl.program_id(0) == 0)
        def _():
            tile = [(s_ref[s, 0, 0], -s_ref[s, 0, 1]) for s in range(groups)]
            x_radix(tile, z, 0, turn_ref, lanes, SUB)
            zq[:small, :] = data_table(z[:small, :], wx_ref)
            for t in range(groups):
                at = slice(t * SUB, t * SUB + 1)
                cols = slice(t * lanes, (t + 1) * lanes)
                zr, zi = zq[at, :lanes], zq[at, lanes:]
                kr, ki = b_ref[0, :, cols], b_ref[1, :, cols]
                re, im = zr * kr + zi * ki, zi * kr - zr * ki
                for d in range(depth):
                    top = slice(d * block + t * pair, d * block + t * pair + 1)
                    c_s[top, :lanes] += re[d:d + 1, :]
                    c_s[top, lanes:] += im[d:d + 1, :]

        for d in range(depth):
            zc[d * block:(d + 1) * block, :] = data_table(c_s[d * block:(d + 1) * block, :], wxi_ref)

        def back(i, carry):
            d, h = i // 2, i % 2
            j = pl.program_id(0) * 2 + h
            out = x_unradix(zc, d * block + h * SUB, turn_ref, groups, lanes, pair)
            for s, (re, im) in enumerate(out):
                o_ref[s, d, j, 0] = re
                o_ref[s, d, j, 1] = im
            return carry

        lax.fori_loop(0, 2 * depth, back, 0)

    outgoing = pl.pallas_call(
        correct_kernel,
        grid=(tiles // 2,),
        in_specs=[near] * 6,
        out_specs=near,
        out_shape=pltpu.VMEM(many(depth), f32),
        scratch_shapes=[x_scratch(1), x_scratch(1), x_scratch(depth), x_scratch(depth)],
        compiler_params=pltpu.CompilerParams(vmem_limit_bytes=24 << 20),
        name="correct_x",
    )(*x_near, keep(arrived), keep(a_all), keep(b_all))
    arrived = swap(outgoing)

    def final_kernel(wy_ref, w0_ref, turn_ref, g_ref, v_ref, o_ref, z):
        def fetch(t):
            return g_ref[:, pl.program_id(0), t].reshape(groups * 2 * SUB, rows)

        def write(i, here, outs):
            for a, value in enumerate(outs):
                cols = slice(a * lanes, (a + 1) * lanes)
                o_ref[0, here, cols] = v_ref[pl.program_id(0), here, cols] * value

        y_inverse(fetch, write, z, wy_ref, w0_ref, turn_ref, groups, rows, lanes)

    new_volume = pl.pallas_call(
        final_kernel,
        grid=(depth,),
        in_specs=[near] * 3 + [near, near],
        out_specs=pl.BlockSpec((1, rows, length), lambda d: (d, 0, 0)),
        out_shape=jax.ShapeDtypeStruct((depth, rows, length), f32),
        scratch_shapes=[y_scratch],
        compiler_params=pltpu.CompilerParams(vmem_limit_bytes=16 << 20),
        name="final_y",
    )(*y_near, keep(arrived), keep(volume))
    return new_volume, projection


def solution(mesh):
    groups, parts = mesh.shape["row"], mesh.shape["vol"]

    def shards(volume, psf_spectra, background, measured):
        rows = volume.shape[1]
        fits = parts == 2 and rows == LANES and rows == SUB * groups
        body = fast_shards if fits else generic_shards
        return body(volume, psf_spectra, background, measured)

    in_specs = (
        P("vol", "row", None),
        P(None, None, "row", None),
        P("row", None),
        P(("vol", "row"), None),
    )
    out_specs = (P("vol", "row", None), P(("vol", "row"), None))
    return jax.shard_map(shards, mesh=mesh, in_specs=in_specs, out_specs=out_specs, check_vma=False)
```

```python
import math

import jax
import jax.numpy as jnp
import numpy as np
from jax import lax
from jax.experimental import pallas as pl
from jax.experimental.pallas import tpu as pltpu
from jax.sharding import PartitionSpec as P


FLOOR = 0.5
HIGHEST = lax.Precision.HIGHEST
LANES = 128
SUB = 8


def phase_pair(first_extent, second_extent, modulus, direction):
    first_idx = jnp.arange(first_extent, dtype=jnp.int32)
    second_idx = jnp.arange(second_extent, dtype=jnp.int32)
    phases = first_idx[:, None] * second_idx[None, :] % modulus
    angles = phases.astype(jnp.float32) * (2.0 * math.pi / modulus)
    return (jnp.cos(angles), direction * jnp.sin(angles))


def contract(pattern, fields, coeffs, real_only):
    real_part, imag_part = fields
    coeff_real, coeff_imag = coeffs

    def product(operand, table_side):
        return jnp.einsum(pattern, operand, table_side, precision=HIGHEST)

    if imag_part is None:
        return (product(real_part, coeff_real), product(real_part, coeff_imag))
    out_real = product(real_part, coeff_real) - product(imag_part, coeff_imag)
    if real_only:
        return (out_real, None)
    return (out_real, product(real_part, coeff_imag) + product(imag_part, coeff_real))


def rotate(fields, factors):
    real_part, imag_part = fields
    factor_real, factor_imag = factors
    return (
        real_part * factor_real - imag_part * factor_imag,
        real_part * factor_imag + imag_part * factor_real,
    )


def leading_pass(fields, groups, direction):
    batch_size, row_count, length = fields[0].shape
    inner_count = length // groups
    shaped = tuple(
        None if member is None else member.reshape(batch_size, row_count, inner_count, groups)
        for member in fields
    )
    sectioned = contract(
        "bqnm,nk->bqkm", shaped, phase_pair(inner_count, inner_count, inner_count, direction), False
    )
    sectioned = rotate(sectioned, phase_pair(inner_count, groups, length, direction))
    sectioned = contract(
        "bqkm,mp->bpkq", sectioned, phase_pair(groups, groups, groups, direction), False
    )
    return tuple(member.reshape(batch_size, groups, inner_count * row_count) for member in sectioned)


def trailing_pass(fields, row_count, direction, real_only):
    batch_size, groups, merged = fields[0].shape
    inner_count = merged // row_count
    length = groups * row_count
    shaped = tuple(member.reshape(batch_size, groups, inner_count, row_count) for member in fields)
    sectioned = contract(
        "bskq,st->bktq", shaped, phase_pair(groups, groups, groups, direction), False
    )
    sectioned = rotate(sectioned, phase_pair(groups, row_count, length, direction))
    sectioned = contract(
        "bktq,qu->bkut", sectioned, phase_pair(row_count, row_count, row_count, direction), real_only
    )
    return tuple(
        None if member is None else member.reshape(batch_size, inner_count, length)
        for member in sectioned
    )


def generic_shards(volume, psf_spectra, background, measured):
    groups = lax.axis_size("row")
    row_count = volume.shape[1]
    length = volume.shape[2]
    inverse_scale = 1.0 / (length * length)
    response_real = psf_spectra[0].astype(jnp.float32)
    response_imag = psf_spectra[1].astype(jnp.float32)

    def swap(field):
        return lax.all_to_all(field, "row", split_axis=1, concat_axis=1, tiled=True)

    outgoing = leading_pass((volume, None), groups, -1.0)
    spec_real, spec_imag = trailing_pass(
        (swap(outgoing[0]), swap(outgoing[1])), row_count, -1.0, False
    )
    prod_real = spec_real * response_real - spec_imag * response_imag
    prod_imag = spec_real * response_imag + spec_imag * response_real
    summed = (jnp.sum(prod_real, axis=0, keepdims=True), jnp.sum(prod_imag, axis=0, keepdims=True))
    outgoing = leading_pass(summed, groups, 1.0)
    arrived = (swap(outgoing[0]), swap(outgoing[1]))
    projection = trailing_pass(arrived, row_count, 1.0, True)[0][0] * inverse_scale
    quotient = measured / jnp.maximum(projection + background, FLOOR)
    outgoing = leading_pass((quotient[None], None), groups, -1.0)
    arrived = (swap(outgoing[0]), swap(outgoing[1]))
    ratio_real, ratio_imag = trailing_pass(arrived, row_count, -1.0, False)
    corr_real = ratio_real * response_real + ratio_imag * response_imag
    corr_imag = ratio_imag * response_real - ratio_real * response_imag
    outgoing = leading_pass((corr_real, corr_imag), groups, 1.0)
    arrived = (swap(outgoing[0]), swap(outgoing[1]))
    correction = trailing_pass(arrived, row_count, 1.0, True)[0] * inverse_scale
    return (volume * correction, projection)


def times(z, angle):
    re, im = z
    c, s = math.cos(angle), math.sin(angle)
    if abs(s) < 1e-12:
        return z if c > 0 else (-re, None if im is None else -im)
    if abs(c) < 1e-12:
        if im is None:
            return (None, re if s > 0 else -re)
        return (-im, re) if s > 0 else (im, -re)
    if im is None:
        return (re * c, re * s)
    if abs(abs(c) - abs(s)) < 1e-12:
        sc, ss = math.copysign(1.0, c), math.copysign(1.0, s)
        a = re if sc > 0 else -re
        b = im if sc > 0 else -im
        r, i = (a - im, b + re) if ss > 0 else (a + im, b - re)
        return (r * abs(c), i * abs(c))
    return (re * c - im * s, re * s + im * c)


def plus(a, b):
    if a is None:
        return b
    return a if b is None else a + b


def minus(a, b):
    if b is None:
        return a
    return -b if a is None else a - b


def cadd(a, b):
    return (plus(a[0], b[0]), plus(a[1], b[1]))


def csub(a, b):
    return (minus(a[0], b[0]), minus(a[1], b[1]))


def conj(a):
    return (a[0], None if a[1] is None else -a[1])


def cfft(xs, sign):
    n = len(xs)
    if n == 1:
        return list(xs)
    even, odd = cfft(xs[0::2], sign), cfft(xs[1::2], sign)
    turned = [times(odd[t], sign * 2.0 * math.pi * t / n) for t in range(n // 2)]
    return [cadd(even[t], turned[t]) for t in range(n // 2)] + [
        csub(even[t], turned[t]) for t in range(n // 2)
    ]


def rfft(xs):
    n = len(xs)
    if n == 2:
        return [(xs[0] + xs[1], None), (xs[0] - xs[1], None)]
    even, odd = rfft(xs[0::2]), rfft(xs[1::2])
    out = [None] * (n // 2 + 1)
    for t in range(n // 4 + 1):
        turned = times(odd[t], -2.0 * math.pi * t / n)
        out[t] = cadd(even[t], turned)
        if t < n // 4:
            out[n // 2 - t] = conj(csub(even[t], turned))
    return out


def c2r(zs):
    n = 2 * (len(zs) - 1)
    if n == 2:
        return [zs[0][0] + zs[1][0], zs[0][0] - zs[1][0]]
    q = n // 4
    even, odd = [], []
    for t in range(q):
        mirror = conj(zs[n // 2 - t])
        even.append(cadd(zs[t], mirror))
        odd.append(times(csub(zs[t], mirror), 2.0 * math.pi * t / n))
    even.append((zs[q][0] * 2.0, None))
    odd.append((zs[q][1] * -2.0, None))
    a, b = c2r(even), c2r(odd)
    return [half[i] for i in range(n // 2) for half in (a, b)]


def split_table(table):
    high = table.astype(jnp.bfloat16)
    low = (table - high.astype(np.float64)).astype(jnp.bfloat16)
    return np.stack([high, low])


def make_tables(groups, lanes):
    length = groups * lanes
    per = lanes // groups
    pos = np.arange(lanes)
    w_y = np.zeros((groups, 2, SUB, 2, lanes))
    w_0 = np.zeros((groups, 2, SUB, 2, lanes))
    half = SUB // 2
    for p in range(groups):
        for r in range(SUB):
            ang = 2.0 * np.pi * ((per * p + r) * pos % lanes) / lanes
            w_y[p, 0, r] = np.cos(ang), np.sin(ang)
            w_y[p, 1, r] = -np.sin(ang), np.cos(ang)
            if r < half:
                unit = per * p + r
                if r == 0 and p >= groups // 2:
                    unit = per * p + per // 2
                ang = 2.0 * np.pi * (groups * unit * pos % length) / length
                w_0[p, 0, r, 0] = np.cos(ang)
                w_0[p, 1, r, 0] = -np.sin(ang)
                if r == 0 and p == 0:
                    w_0[p, 1, r, 0] = (-1.0) ** pos
            else:
                ang = (groups * (per * p + r - half) + groups // 2) * pos % length
                ang = 2.0 * np.pi * ang / length
                w_0[p, 0, r, 1] = np.cos(ang)
                w_0[p, 1, r, 1] = -np.sin(ang)
    rows = groups * 2 * SUB
    ang = 2.0 * np.pi * (pos[:, None] * pos[None, :] % lanes) / lanes
    w_x = np.block([[np.cos(ang), -np.sin(ang)], [np.sin(ang), np.cos(ang)]])
    ang = 2.0 * np.pi * (np.arange(groups)[:, None] * pos[None, :] % length) / length
    turn = np.stack([np.cos(ang), -np.sin(ang)], axis=1).astype(np.float32)
    w_y, w_0 = split_table(w_y.reshape(rows, 2 * lanes)), split_table(w_0.reshape(rows, 2 * lanes))
    return w_y, w_0, split_table(w_x), split_table(w_x.T), turn


def kept_rows(groups, lanes):
    per = lanes // groups
    half = SUB // 2
    own = [groups * w for w in range(half)] + [groups * w + groups // 2 for w in range(half)]
    for tile in range(1, groups // 2):
        own += [groups * w + tile for w in range(per)]
    return own


NN = (((1,), (0,)), ((), ()))
NT = (((1,), (1,)), ((), ()))


def halves(x):
    high = x.astype(jnp.bfloat16)
    return high, (x - high.astype(jnp.float32)).astype(jnp.bfloat16)


def mm(a, b, dims):
    return lax.dot_general(a, b, dims, preferred_element_type=jnp.float32)


def data_table(x, table):
    high, low = halves(x)
    return mm(high, table[0], NN) + (mm(low, table[0], NN) + mm(high, table[1], NN))


def table_data(table, x):
    high, low = halves(x)
    return mm(table[0], high, NT) + (mm(table[0], low, NT) + mm(table[1], high, NT))


def y_store(xs, z, here, turn, groups, lanes):
    out = rfft(xs)
    z[0, here, :lanes] = out[0][0]
    z[0, here, lanes:] = out[groups // 2][0]
    for t in range(1, groups // 2):
        re, im = out[t]
        c, s = turn[t, 0:1, :], turn[t, 1:2, :]
        z[t, here, :lanes] = re * c - im * s
        z[t, here, lanes:] = re * s + im * c


def y_forward(read, emit, z, w_y, w_0, turn, groups, rows, lanes):
    def chunk(i, carry):
        here = pl.ds(pl.multiple_of(i * SUB, SUB), SUB)
        y_store([read(i, a) for a in range(groups)], z, here, turn, groups, lanes)
        return carry

    lax.fori_loop(0, rows // SUB, chunk, 0)
    for t in range(groups // 2):
        emit(t, table_data(w_0 if t == 0 else w_y, z[t]))


def y_inverse(fetch, write, z, w_y, w_0, turn, groups, rows, lanes):
    for t in range(groups // 2):
        z[t] = data_table(fetch(t).T, w_0 if t == 0 else w_y)

    def chunk(i, carry):
        here = pl.ds(pl.multiple_of(i * SUB, SUB), SUB)
        zs = [(z[0, here, :lanes] * 2.0, None)]
        for t in range(1, groups // 2):
            re, im = z[t, here, :lanes], z[t, here, lanes:]
            c, s = turn[t, 0:1, :], turn[t, 1:2, :]
            zs.append((re * c + im * s, im * c - re * s))
        zs.append((z[0, here, lanes:] * 2.0, None))
        write(i, here, c2r(zs))
        return carry

    lax.fori_loop(0, rows // SUB, chunk, 0)


def x_radix(tile, z, base, turn, lanes, step):
    for t, (re, im) in enumerate(cfft(tile, -1.0)):
        here = slice(base + t * step, base + t * step + SUB)
        if t == 0:
            z[here, :lanes] = re
            z[here, lanes:] = im
        else:
            c, s = turn[t, 0:1, :], turn[t, 1:2, :]
            z[here, :lanes] = re * c - im * s
            z[here, lanes:] = re * s + im * c


def x_unradix(z, base, turn, groups, lanes, step):
    zs = []
    for t in range(groups):
        here = slice(base + t * step, base + t * step + SUB)
        re, im = z[here, :lanes], z[here, lanes:]
        if t:
            c, s = turn[t, 0:1, :], turn[t, 1:2, :]
            re, im = re * c + im * s, im * c - re * s
        zs.append((re, im))
    return cfft(zs, 1.0)


def fast_shards(volume, psf_spectra, background, measured):
    groups = lax.axis_size("row")
    depth, rows, length = volume.shape
    lanes = LANES
    tiles = groups // 2
    kept = tiles * SUB
    pair = 2 * SUB
    f32 = jnp.float32
    place = lax.axis_index("row")
    part = lax.axis_index("vol")
    w_y, w_0, w_x, w_xi, turn = (jnp.asarray(t) for t in make_tables(groups, lanes))
    own_rows = kept_rows(groups, rows)

    whole = lambda *shape: pl.BlockSpec(shape, lambda *_: (0,) * len(shape))
    near = pl.BlockSpec(memory_space=pltpu.VMEM)

    def keep(x):
        return pltpu.with_memory_space_constraint(x, pltpu.VMEM)

    def far(x):
        return pltpu.with_memory_space_constraint(x, pltpu.HBM)

    y_tables, x_tables = (w_y, w_0, turn), (w_x, w_xi, turn)
    y_near = tuple(keep(t) for t in (w_y, w_0, turn))
    x_near = tuple(keep(t) for t in x_tables)
    y_specs = [whole(*t.shape) for t in y_tables]
    x_specs = [whole(*t.shape) for t in x_tables]
    y_scratch = pltpu.VMEM((tiles, rows, 2 * lanes), f32)
    send_shape = (groups, tiles, 2, SUB, lanes)

    def many(n):
        return (groups, n, tiles, 2, SUB, lanes)

    low = place < groups // 2
    mid = rows // 2
    pick_send = np.zeros((kept, rows), np.float32)
    pick_own = np.zeros((kept, rows), np.float32)
    for r, k in enumerate(own_rows):
        pick_send[r, (rows - k) if k else mid] = 1.0
        pick_own[r, k] = 1.0
    pick_high = pick_own.copy()
    pick_high[0] = 0.0
    pick_high[0, mid] = 1.0

    def pick_kernel(part_ref, sel_ref, psf_ref, send_ref):
        send_ref[...] = mm(sel_ref[...], psf_ref[0, 0], NN)

    flags = jnp.stack([low.astype(jnp.int32), part.astype(jnp.int32), (place == 0).astype(jnp.int32)])
    smem = pl.BlockSpec(memory_space=pltpu.SMEM)
    bf = jnp.bfloat16
    sel_send = jnp.asarray(pick_send, bf)
    flip = [(p, groups - 1 - p) for p in range(groups)]
    sends, mine, other = [], [], []
    for d in range(depth):
        send = pl.pallas_call(
            pick_kernel,
            grid_spec=pltpu.PrefetchScalarGridSpec(
                num_scalar_prefetch=1,
                grid=(1,),
                in_specs=[whole(kept, rows),
                          pl.BlockSpec((1, 1, rows, length), lambda i, where, d=d: (where[0], d, 0, 0))],
                out_specs=whole(kept, length),
            ),
            out_shape=jax.ShapeDtypeStruct((kept, length), f32),
            name="pick",
        )(part.astype(jnp.int32).reshape(1), sel_send, psf_spectra)
        sends.append(send)
        mine.append(lax.ppermute(send, "row", flip))
    late, early, _ = lax.optimization_barrier((psf_spectra, volume, sends[-1]))
    edge = late[:, :, 0, :].astype(f32).reshape(2 * depth, length)
    edge = jnp.pad(edge, ((0, pair - 2 * depth), (0, 0)))
    ends = [(groups - p, p) for p in range(1, groups // 2)] + [(groups // 2, 0)]
    edge = lax.ppermute(edge, "row", ends)
    for d in range(depth):
        other.append(lax.ppermute(mine[d], "vol", [(0, 1), (1, 0)]))

    scale = 0.5 / (length * length)
    many_t = 2
    width = many_t * lanes

    def mix_kernel(where_ref, own_l_ref, own_h_ref, psf_ref, edge_ref, *rest):
        mine_refs, other_refs = rest[:depth], rest[depth:2 * depth]
        a_ref, b_ref, o_s, p_s, e_s = rest[2 * depth:]
        step = pl.program_id(0)

        @pl.when(step == 0)
        def _():
            zero = where_ref[2] == 1
            is_low = where_ref[0] == 1
            sel = jnp.where(is_low, own_l_ref[...], own_h_ref[...]).astype(bf)
            first = lax.broadcasted_iota(jnp.int32, (SUB, length), 0) == 0
            for c in range(2):
                mine_here = where_ref[1] == c
                for d in range(depth):
                    row = c * depth + d
                    base = row * kept
                    kept_own = mm(sel, psf_ref[c, d], NN)
                    o_s[base:base + kept, :] = kept_own.astype(bf)
                    p = jnp.where(mine_here, mine_refs[d][...], other_refs[d][...])
                    swap = jnp.where(zero, kept_own[0:1, :], edge_ref[row:row + 1, :])
                    head = jnp.where(jnp.logical_and(first, is_low), swap, p[:SUB])
                    p_s[base:base + kept, :] = jnp.concatenate([head, p[SUB:]], 0).astype(bf)
            e_s[...] = edge_ref[...].astype(bf)

        freq = lax.broadcasted_iota(jnp.int32, (length, width), 0)
        col = lax.broadcasted_iota(jnp.int32, (length, width), 1)
        target = (col % lanes) * groups + step * many_t + col // lanes
        hot = jnp.where(freq == target, 1.0, 0.0).astype(bf)
        hot_rev = jnp.where(freq == (length - target) % length, 1.0, 0.0).astype(bf)
        plain = mm(o_s[...], hot, NN)
        mirror = mm(p_s[...], hot_rev, NN)
        e_plain = mm(e_s[...], hot, NN)
        e_mirror = mm(e_s[...], hot_rev, NN)
        zero = jnp.where(where_ref[2] == 1, 1.0, 0.0).astype(f32)
        b_ref[...] = jnp.zeros((2, SUB, width), f32)
        first = lax.broadcasted_iota(jnp.int32, (SUB, width), 0) == 0
        for c in range(2):
            sign = 1.0 if c == 0 else -1.0
            for d in range(depth):
                row = c * depth + d
                base = row * kept
                h = (plain[base:base + kept] + sign * mirror[base:base + kept]) * scale
                e = (e_plain[row:row + 1] + sign * e_mirror[row:row + 1]) * scale
                a0 = h[:SUB] * (1.0 - 0.75 * zero) + (0.25 * zero) * e
                b0 = (h[:SUB] - e) * (0.25 * zero)
                a_ref[c, d, :SUB, :] = jnp.where(first, a0, h[:SUB])
                a_ref[c, d, SUB:, :] = h[SUB:]
                b_ref[c, d:d + 1, :] = b0[0:1, :]

    planes = 2 * depth * kept
    a_all, b_all = pl.pallas_call(
        mix_kernel,
        grid=(groups // many_t,),
        in_specs=[smem, whole(kept, rows), whole(kept, rows), whole(2, depth, rows, length),
                  whole(pair, length)] + [whole(kept, length)] * (2 * depth),
        out_specs=[pl.BlockSpec((2, depth, kept, width), lambda i: (0, 0, 0, i)),
                   pl.BlockSpec((2, SUB, width), lambda i: (0, 0, i))],
        out_shape=[jax.ShapeDtypeStruct((2, depth, kept, length), f32),
                   jax.ShapeDtypeStruct((2, SUB, length), f32)],
        scratch_shapes=[pltpu.VMEM((planes, length), bf), pltpu.VMEM((planes, length), bf),
                        pltpu.VMEM((pair, length), bf)],
        name="mix",
    )(flags, jnp.asarray(pick_own), jnp.asarray(pick_high), psf_spectra, edge, *mine, *other)

    def forward_kernel(wy_ref, w0_ref, turn_ref, v_ref, o_ref, z):
        def read(i, a):
            return v_ref[0, pl.ds(pl.multiple_of(i * SUB, SUB), SUB), a * lanes:(a + 1) * lanes]

        def emit(t, out):
            o_ref[:, 0, t] = out.reshape(groups, 2, SUB, rows)

        y_forward(read, emit, z, wy_ref, w0_ref, turn_ref, groups, rows, lanes)

    outgoing = pl.pallas_call(
        forward_kernel,
        grid=(depth,),
        in_specs=y_specs + [pl.BlockSpec((1, rows, length), lambda d: (d, 0, 0))],
        out_specs=pl.BlockSpec((groups, 1, tiles, 2, SUB, lanes), lambda d: (0, d, 0, 0, 0, 0)),
        out_shape=jax.ShapeDtypeStruct(many(depth), f32),
        scratch_shapes=[y_scratch],
        name="forward_y",
    )(*y_tables, early)

    def swap(field):
        return lax.all_to_all(field, "row", split_axis=0, concat_axis=0, tiled=True)

    outgoing, _ = lax.optimization_barrier((outgoing, mine[0]))
    arrived = swap(outgoing)

    block = groups * pair
    x_scratch = lambda n: pltpu.VMEM((n * block, 2 * lanes), f32)

    small = groups * SUB
    lead = lambda: lax.broadcasted_iota(jnp.int32, (SUB, lanes), 0)

    def project_kernel(wx_ref, wxi_ref, turn_ref, s_ref, a_ref, b_ref, o_ref, z, t_s, zc):
        for d in range(depth):
            for h in range(2):
                j = pl.program_id(0) * 2 + h
                tile = [(s_ref[s, d, j, 0], s_ref[s, d, j, 1]) for s in range(groups)]
                x_radix(tile, z, d * block + h * SUB, turn_ref, lanes, pair)
            zc[d * block:(d + 1) * block, :] = data_table(z[d * block:(d + 1) * block, :], wx_ref)
        for t in range(groups):
            here = slice(t * pair, (t + 1) * pair)
            cols = slice(t * lanes, (t + 1) * lanes)
            re = im = None
            for d in range(depth):
                at = slice(d * block + t * pair, d * block + (t + 1) * pair)
                zr, zi = zc[at, :lanes], zc[at, lanes:]
                kr, ki = a_ref[0, d, :, cols], a_ref[1, d, :, cols]
                re = plus(re, zr * kr - zi * ki)
                im = plus(im, zr * ki + zi * kr)
            t_s[here, :lanes] = re
            t_s[here, lanes:] = im

        @pl.when(pl.program_id(0) == 0)
        def _():
            def row(s, c):
                out = s_ref[s, 0, 0, c, 0:1, :]
                for d in range(1, depth):
                    out = jnp.where(lead() == d, s_ref[s, d, 0, c, 0:1, :], out)
                return jnp.broadcast_to(out, (SUB, lanes))

            x_radix([(row(s, 0), -row(s, 1)) for s in range(groups)], z, 0, turn_ref, lanes, SUB)
            zc[:small, :] = data_table(z[:small, :], wx_ref)
            for t in range(groups):
                at = slice(t * SUB, (t + 1) * SUB)
                cols = slice(t * lanes, (t + 1) * lanes)
                zr, zi = zc[at, :lanes], zc[at, lanes:]
                kr, ki = b_ref[0, :, cols], b_ref[1, :, cols]
                top = slice(t * pair, t * pair + 1)
                t_s[top, :lanes] += jnp.sum(zr * kr - zi * ki, axis=0, keepdims=True)
                t_s[top, lanes:] += jnp.sum(zr * ki + zi * kr, axis=0, keepdims=True)

        zc[:block, :] = data_table(t_s[...], wxi_ref)

        for h in range(2):
            j = pl.program_id(0) * 2 + h
            for s, (re, im) in enumerate(x_unradix(zc, h * SUB, turn_ref, groups, lanes, pair)):
                o_ref[s, j, 0] = re
                o_ref[s, j, 1] = im

    k_specs = [pl.BlockSpec((2, depth, pair, length), lambda j: (0, 0, j, 0)), whole(2, SUB, length)]
    outgoing = pl.pallas_call(
        project_kernel,
        grid=(tiles // 2,),
        in_specs=x_specs + [near] + k_specs,
        out_specs=near,
        out_shape=pltpu.VMEM(send_shape, f32),
        scratch_shapes=[x_scratch(depth), x_scratch(1), x_scratch(depth)],
        compiler_params=pltpu.CompilerParams(vmem_limit_bytes=24 << 20),
        name="project_x",
    )(*(far(t) for t in x_tables), keep(arrived), far(a_all), far(b_all))
    arrived = swap(outgoing)

    def ratio_kernel(wy_ref, w0_ref, turn_ref, g_ref, bg_ref, me_ref, p_ref, o_ref, z):
        def fetch(t):
            return g_ref[:, t].reshape(groups * 2 * SUB, rows)

        def write(i, here, outs):
            ratio = []
            for a, value in enumerate(outs):
                cols = slice(a * lanes, (a + 1) * lanes)
                p_ref[here, cols] = value
                ratio.append(me_ref[here, cols] / jnp.maximum(value + bg_ref[here, cols], FLOOR))
            y_store(ratio, z, here, turn_ref, groups, lanes)

        y_inverse(fetch, write, z, wy_ref, w0_ref, turn_ref, groups, rows, lanes)
        for t in range(tiles):
            out = table_data(w0_ref if t == 0 else wy_ref, z[t])
            o_ref[:, t] = out.reshape(groups, 2, SUB, rows)

    projection, outgoing = pl.pallas_call(
        ratio_kernel,
        in_specs=[near] * 6,
        out_specs=[whole(rows, length), near],
        out_shape=[jax.ShapeDtypeStruct((rows, length), f32), pltpu.VMEM(send_shape, f32)],
        scratch_shapes=[y_scratch],
        compiler_params=pltpu.CompilerParams(vmem_limit_bytes=16 << 20),
        name="ratio",
    )(*y_near, keep(arrived), keep(background), keep(measured))
    arrived = swap(outgoing)

    def correct_kernel(wx_ref, wxi_ref, turn_ref, s_ref, a_ref, b_ref, o_ref, z, zq, zc, c_s):
        mine_rows = pl.ds(pl.multiple_of(pl.program_id(0) * pair, pair), pair)

        for h in range(2):
            j = pl.program_id(0) * 2 + h
            tile = [(s_ref[s, j, 0], s_ref[s, j, 1]) for s in range(groups)]
            x_radix(tile, z, h * SUB, turn_ref, lanes, pair)
        zq[...] = data_table(z[...], wx_ref)
        for t in range(groups):
            here = slice(t * pair, (t + 1) * pair)
            cols = slice(t * lanes, (t + 1) * lanes)
            zr, zi = zq[here, :lanes], zq[here, lanes:]
            for d in range(depth):
                at = slice(d * block + t * pair, d * block + (t + 1) * pair)
                kr, ki = a_ref[0, d, mine_rows, cols], a_ref[1, d, mine_rows, cols]
                c_s[at, :lanes] = zr * kr + zi * ki
                c_s[at, lanes:] = zi * kr - zr * ki

        @pl.when(pl.program_id(0) == 0)
        def _():
            tile = [(s_ref[s, 0, 0], -s_ref[s, 0, 1]) for s in range(groups)]
            x_radix(tile, z, 0, turn_ref, lanes, SUB)
            zq[:small, :] = data_table(z[:small, :], wx_ref)
            for t in range(groups):
                at = slice(t * SUB, t * SUB + 1)
                cols = slice(t * lanes, (t + 1) * lanes)
                zr, zi = zq[at, :lanes], zq[at, lanes:]
                kr, ki = b_ref[0, :, cols], b_ref[1, :, cols]
                re, im = zr * kr + zi * ki, zi * kr - zr * ki
                for d in range(depth):
                    top = slice(d * block + t * pair, d * block + t * pair + 1)
                    c_s[top, :lanes] += re[d:d + 1, :]
                    c_s[top, lanes:] += im[d:d + 1, :]

        for d in range(depth):
            zc[d * block:(d + 1) * block, :] = data_table(c_s[d * block:(d + 1) * block, :], wxi_ref)
            for h in range(2):
                j = pl.program_id(0) * 2 + h
                out = x_unradix(zc, d * block + h * SUB, turn_ref, groups, lanes, pair)
                for s, (re, im) in enumerate(out):
                    o_ref[s, d, j, 0] = re
                    o_ref[s, d, j, 1] = im

    outgoing = pl.pallas_call(
        correct_kernel,
        grid=(tiles // 2,),
        in_specs=[near] * 6,
        out_specs=near,
        out_shape=pltpu.VMEM(many(depth), f32),
        scratch_shapes=[x_scratch(1), x_scratch(1), x_scratch(depth), x_scratch(depth)],
        compiler_params=pltpu.CompilerParams(vmem_limit_bytes=24 << 20),
        name="correct_x",
    )(*x_near, keep(arrived), keep(a_all), keep(b_all))
    arrived = swap(outgoing)

    def final_kernel(wy_ref, w0_ref, turn_ref, g_ref, v_ref, o_ref, z):
        def fetch(t):
            return g_ref[:, pl.program_id(0), t].reshape(groups * 2 * SUB, rows)

        def write(i, here, outs):
            for a, value in enumerate(outs):
                cols = slice(a * lanes, (a + 1) * lanes)
                o_ref[0, here, cols] = v_ref[pl.program_id(0), here, cols] * value

        y_inverse(fetch, write, z, wy_ref, w0_ref, turn_ref, groups, rows, lanes)

    new_volume = pl.pallas_call(
        final_kernel,
        grid=(depth,),
        in_specs=[near] * 3 + [near, near],
        out_specs=pl.BlockSpec((1, rows, length), lambda d: (d, 0, 0)),
        out_shape=jax.ShapeDtypeStruct((depth, rows, length), f32),
        scratch_shapes=[y_scratch],
        compiler_params=pltpu.CompilerParams(vmem_limit_bytes=16 << 20),
        name="final_y",
    )(*y_near, keep(arrived), keep(volume))
    return new_volume, projection


def solution(mesh):
    groups, parts = mesh.shape["row"], mesh.shape["vol"]

    def shards(volume, psf_spectra, background, measured):
        rows = volume.shape[1]
        fits = parts == 2 and rows == LANES and rows == SUB * groups
        body = fast_shards if fits else generic_shards
        return body(volume, psf_spectra, background, measured)

    in_specs = (
        P("vol", "row", None),
        P(None, None, "row", None),
        P("row", None),
        P(("vol", "row"), None),
    )
    out_specs = (P("vol", "row", None), P(("vol", "row"), None))
    return jax.shard_map(shards, mesh=mesh, in_specs=in_specs, out_specs=out_specs, check_vma=False)
```

```python
import math

import jax
import jax.numpy as jnp
import numpy as np
from jax import lax
from jax.experimental import pallas as pl
from jax.experimental.pallas import tpu as pltpu
from jax.sharding import PartitionSpec as P


FLOOR = 0.5
HIGHEST = lax.Precision.HIGHEST
LANES = 128
SUB = 8


def phase_pair(first_extent, second_extent, modulus, direction):
    first_idx = jnp.arange(first_extent, dtype=jnp.int32)
    second_idx = jnp.arange(second_extent, dtype=jnp.int32)
    phases = first_idx[:, None] * second_idx[None, :] % modulus
    angles = phases.astype(jnp.float32) * (2.0 * math.pi / modulus)
    return (jnp.cos(angles), direction * jnp.sin(angles))


def contract(pattern, fields, coeffs, real_only):
    real_part, imag_part = fields
    coeff_real, coeff_imag = coeffs

    def product(operand, table_side):
        return jnp.einsum(pattern, operand, table_side, precision=HIGHEST)

    if imag_part is None:
        return (product(real_part, coeff_real), product(real_part, coeff_imag))
    out_real = product(real_part, coeff_real) - product(imag_part, coeff_imag)
    if real_only:
        return (out_real, None)
    return (out_real, product(real_part, coeff_imag) + product(imag_part, coeff_real))


def rotate(fields, factors):
    real_part, imag_part = fields
    factor_real, factor_imag = factors
    return (
        real_part * factor_real - imag_part * factor_imag,
        real_part * factor_imag + imag_part * factor_real,
    )


def leading_pass(fields, groups, direction):
    batch_size, row_count, length = fields[0].shape
    inner_count = length // groups
    shaped = tuple(
        None if member is None else member.reshape(batch_size, row_count, inner_count, groups)
        for member in fields
    )
    sectioned = contract(
        "bqnm,nk->bqkm", shaped, phase_pair(inner_count, inner_count, inner_count, direction), False
    )
    sectioned = rotate(sectioned, phase_pair(inner_count, groups, length, direction))
    sectioned = contract(
        "bqkm,mp->bpkq", sectioned, phase_pair(groups, groups, groups, direction), False
    )
    return tuple(member.reshape(batch_size, groups, inner_count * row_count) for member in sectioned)


def trailing_pass(fields, row_count, direction, real_only):
    batch_size, groups, merged = fields[0].shape
    inner_count = merged // row_count
    length = groups * row_count
    shaped = tuple(member.reshape(batch_size, groups, inner_count, row_count) for member in fields)
    sectioned = contract(
        "bskq,st->bktq", shaped, phase_pair(groups, groups, groups, direction), False
    )
    sectioned = rotate(sectioned, phase_pair(groups, row_count, length, direction))
    sectioned = contract(
        "bktq,qu->bkut", sectioned, phase_pair(row_count, row_count, row_count, direction), real_only
    )
    return tuple(
        None if member is None else member.reshape(batch_size, inner_count, length)
        for member in sectioned
    )


def generic_shards(volume, psf_spectra, background, measured):
    groups = lax.axis_size("row")
    row_count = volume.shape[1]
    length = volume.shape[2]
    inverse_scale = 1.0 / (length * length)
    response_real = psf_spectra[0].astype(jnp.float32)
    response_imag = psf_spectra[1].astype(jnp.float32)

    def swap(field):
        return lax.all_to_all(field, "row", split_axis=1, concat_axis=1, tiled=True)

    outgoing = leading_pass((volume, None), groups, -1.0)
    spec_real, spec_imag = trailing_pass(
        (swap(outgoing[0]), swap(outgoing[1])), row_count, -1.0, False
    )
    prod_real = spec_real * response_real - spec_imag * response_imag
    prod_imag = spec_real * response_imag + spec_imag * response_real
    summed = (jnp.sum(prod_real, axis=0, keepdims=True), jnp.sum(prod_imag, axis=0, keepdims=True))
    outgoing = leading_pass(summed, groups, 1.0)
    arrived = (swap(outgoing[0]), swap(outgoing[1]))
    projection = trailing_pass(arrived, row_count, 1.0, True)[0][0] * inverse_scale
    quotient = measured / jnp.maximum(projection + background, FLOOR)
    outgoing = leading_pass((quotient[None], None), groups, -1.0)
    arrived = (swap(outgoing[0]), swap(outgoing[1]))
    ratio_real, ratio_imag = trailing_pass(arrived, row_count, -1.0, False)
    corr_real = ratio_real * response_real + ratio_imag * response_imag
    corr_imag = ratio_imag * response_real - ratio_real * response_imag
    outgoing = leading_pass((corr_real, corr_imag), groups, 1.0)
    arrived = (swap(outgoing[0]), swap(outgoing[1]))
    correction = trailing_pass(arrived, row_count, 1.0, True)[0] * inverse_scale
    return (volume * correction, projection)


def times(z, angle):
    re, im = z
    c, s = math.cos(angle), math.sin(angle)
    if abs(s) < 1e-12:
        return z if c > 0 else (-re, None if im is None else -im)
    if abs(c) < 1e-12:
        if im is None:
            return (None, re if s > 0 else -re)
        return (-im, re) if s > 0 else (im, -re)
    if im is None:
        return (re * c, re * s)
    if abs(abs(c) - abs(s)) < 1e-12:
        sc, ss = math.copysign(1.0, c), math.copysign(1.0, s)
        a = re if sc > 0 else -re
        b = im if sc > 0 else -im
        r, i = (a - im, b + re) if ss > 0 else (a + im, b - re)
        return (r * abs(c), i * abs(c))
    return (re * c - im * s, re * s + im * c)


def plus(a, b):
    if a is None:
        return b
    return a if b is None else a + b


def minus(a, b):
    if b is None:
        return a
    return -b if a is None else a - b


def cadd(a, b):
    return (plus(a[0], b[0]), plus(a[1], b[1]))


def csub(a, b):
    return (minus(a[0], b[0]), minus(a[1], b[1]))


def conj(a):
    return (a[0], None if a[1] is None else -a[1])


def cfft(xs, sign):
    n = len(xs)
    if n == 1:
        return list(xs)
    even, odd = cfft(xs[0::2], sign), cfft(xs[1::2], sign)
    turned = [times(odd[t], sign * 2.0 * math.pi * t / n) for t in range(n // 2)]
    return [cadd(even[t], turned[t]) for t in range(n // 2)] + [
        csub(even[t], turned[t]) for t in range(n // 2)
    ]


def rfft(xs):
    n = len(xs)
    if n == 2:
        return [(xs[0] + xs[1], None), (xs[0] - xs[1], None)]
    even, odd = rfft(xs[0::2]), rfft(xs[1::2])
    out = [None] * (n // 2 + 1)
    for t in range(n // 4 + 1):
        turned = times(odd[t], -2.0 * math.pi * t / n)
        out[t] = cadd(even[t], turned)
        if t < n // 4:
            out[n // 2 - t] = conj(csub(even[t], turned))
    return out


def c2r(zs):
    n = 2 * (len(zs) - 1)
    if n == 2:
        return [zs[0][0] + zs[1][0], zs[0][0] - zs[1][0]]
    q = n // 4
    even, odd = [], []
    for t in range(q):
        mirror = conj(zs[n // 2 - t])
        even.append(cadd(zs[t], mirror))
        odd.append(times(csub(zs[t], mirror), 2.0 * math.pi * t / n))
    even.append((zs[q][0] * 2.0, None))
    odd.append((zs[q][1] * -2.0, None))
    a, b = c2r(even), c2r(odd)
    return [half[i] for i in range(n // 2) for half in (a, b)]


def split_table(table):
    high = table.astype(jnp.bfloat16)
    low = (table - high.astype(np.float64)).astype(jnp.bfloat16)
    return np.stack([high, low])


def make_tables(groups, lanes):
    length = groups * lanes
    per = lanes // groups
    pos = np.arange(lanes)
    w_y = np.zeros((groups, 2, SUB, 2, lanes))
    w_0 = np.zeros((groups, 2, SUB, 2, lanes))
    half = SUB // 2
    for p in range(groups):
        for r in range(SUB):
            ang = 2.0 * np.pi * ((per * p + r) * pos % lanes) / lanes
            w_y[p, 0, r] = np.cos(ang), np.sin(ang)
            w_y[p, 1, r] = -np.sin(ang), np.cos(ang)
            if r < half:
                unit = per * p + r
                if r == 0 and p >= groups // 2:
                    unit = per * p + per // 2
                ang = 2.0 * np.pi * (groups * unit * pos % length) / length
                w_0[p, 0, r, 0] = np.cos(ang)
                w_0[p, 1, r, 0] = -np.sin(ang)
                if r == 0 and p == 0:
                    w_0[p, 1, r, 0] = (-1.0) ** pos
            else:
                ang = (groups * (per * p + r - half) + groups // 2) * pos % length
                ang = 2.0 * np.pi * ang / length
                w_0[p, 0, r, 1] = np.cos(ang)
                w_0[p, 1, r, 1] = -np.sin(ang)
    rows = groups * 2 * SUB
    ang = 2.0 * np.pi * (pos[:, None] * pos[None, :] % lanes) / lanes
    w_x = np.block([[np.cos(ang), -np.sin(ang)], [np.sin(ang), np.cos(ang)]])
    ang = 2.0 * np.pi * (np.arange(groups)[:, None] * pos[None, :] % length) / length
    turn = np.stack([np.cos(ang), -np.sin(ang)], axis=1).astype(np.float32)
    w_y, w_0 = split_table(w_y.reshape(rows, 2 * lanes)), split_table(w_0.reshape(rows, 2 * lanes))
    return w_y, w_0, split_table(w_x), split_table(w_x.T), turn


def kept_rows(groups, lanes):
    per = lanes // groups
    half = SUB // 2
    own = [groups * w for w in range(half)] + [groups * w + groups // 2 for w in range(half)]
    for tile in range(1, groups // 2):
        own += [groups * w + tile for w in range(per)]
    return own


NN = (((1,), (0,)), ((), ()))
NT = (((1,), (1,)), ((), ()))


def halves(x):
    high = x.astype(jnp.bfloat16)
    return high, (x - high.astype(jnp.float32)).astype(jnp.bfloat16)


def mm(a, b, dims):
    return lax.dot_general(a, b, dims, preferred_element_type=jnp.float32)


def data_table(x, table):
    high, low = halves(x)
    return mm(high, table[0], NN) + (mm(low, table[0], NN) + mm(high, table[1], NN))


def table_data(table, x):
    high, low = halves(x)
    return mm(table[0], high, NT) + (mm(table[0], low, NT) + mm(table[1], high, NT))


def y_store(xs, z, here, turn, groups, lanes):
    out = rfft(xs)
    z[0, here, :lanes] = out[0][0]
    z[0, here, lanes:] = out[groups // 2][0]
    for t in range(1, groups // 2):
        re, im = out[t]
        c, s = turn[t, 0:1, :], turn[t, 1:2, :]
        z[t, here, :lanes] = re * c - im * s
        z[t, here, lanes:] = re * s + im * c


def y_forward(read, emit, z, w_y, w_0, turn, groups, rows, lanes):
    def chunk(i, carry):
        here = pl.ds(pl.multiple_of(i * SUB, SUB), SUB)
        y_store([read(i, a) for a in range(groups)], z, here, turn, groups, lanes)
        return carry

    lax.fori_loop(0, rows // SUB, chunk, 0)
    for t in range(groups // 2):
        emit(t, table_data(w_0 if t == 0 else w_y, z[t]))


def y_load(z, here, turn, groups, lanes):
    zs = [(z[0, here, :lanes] * 2.0, None)]
    for t in range(1, groups // 2):
        re, im = z[t, here, :lanes], z[t, here, lanes:]
        c, s = turn[t, 0:1, :], turn[t, 1:2, :]
        zs.append((re * c + im * s, im * c - re * s))
    zs.append((z[0, here, lanes:] * 2.0, None))
    return zs


def y_inverse(fetch, write, z, w_y, w_0, turn, groups, rows, lanes):
    for t in range(groups // 2):
        z[t] = data_table(fetch(t).T, w_0 if t == 0 else w_y)
    for i in range(rows // SUB):
        here = slice(i * SUB, (i + 1) * SUB)
        write(here, c2r(y_load(z, here, turn, groups, lanes)))


def x_radix(tile, z, base, turn, lanes, step):
    for t, (re, im) in enumerate(cfft(tile, -1.0)):
        here = slice(base + t * step, base + t * step + SUB)
        if t == 0:
            z[here, :lanes] = re
            z[here, lanes:] = im
        else:
            c, s = turn[t, 0:1, :], turn[t, 1:2, :]
            z[here, :lanes] = re * c - im * s
            z[here, lanes:] = re * s + im * c


def x_unradix(z, base, turn, groups, lanes, step):
    zs = []
    for t in range(groups):
        here = slice(base + t * step, base + t * step + SUB)
        re, im = z[here, :lanes], z[here, lanes:]
        if t:
            c, s = turn[t, 0:1, :], turn[t, 1:2, :]
            re, im = re * c + im * s, im * c - re * s
        zs.append((re, im))
    return cfft(zs, 1.0)


def fast_shards(volume, psf_spectra, background, measured):
    groups = lax.axis_size("row")
    depth, rows, length = volume.shape
    lanes = LANES
    tiles = groups // 2
    kept = tiles * SUB
    pair = 2 * SUB
    f32 = jnp.float32
    place = lax.axis_index("row")
    part = lax.axis_index("vol")
    w_y, w_0, w_x, w_xi, turn = (jnp.asarray(t) for t in make_tables(groups, lanes))
    own_rows = kept_rows(groups, rows)

    whole = lambda *shape: pl.BlockSpec(shape, lambda *_: (0,) * len(shape))
    near = pl.BlockSpec(memory_space=pltpu.VMEM)

    def keep(x):
        return pltpu.with_memory_space_constraint(x, pltpu.VMEM)

    def far(x):
        return pltpu.with_memory_space_constraint(x, pltpu.HBM)

    y_tables, x_tables = (w_y, w_0, turn), (w_x, w_xi, turn)
    y_near = tuple(keep(t) for t in (w_y, w_0, turn))
    x_near = tuple(keep(t) for t in x_tables)
    y_specs = [whole(*t.shape) for t in y_tables]
    x_specs = [whole(*t.shape) for t in x_tables]
    y_scratch = pltpu.VMEM((tiles, rows, 2 * lanes), f32)
    send_shape = (groups, tiles, 2, SUB, lanes)

    def many(n):
        return (groups, n, tiles, 2, SUB, lanes)

    low = place < groups // 2
    mid = rows // 2
    pick_send = np.zeros((kept, rows), np.float32)
    pick_own = np.zeros((kept, rows), np.float32)
    for r, k in enumerate(own_rows):
        pick_send[r, (rows - k) if k else mid] = 1.0
        pick_own[r, k] = 1.0
    pick_high = pick_own.copy()
    pick_high[0] = 0.0
    pick_high[0, mid] = 1.0

    def pick_kernel(part_ref, sel_ref, psf_ref, send_ref):
        send_ref[...] = mm(sel_ref[...], psf_ref[0, 0], NN)

    flags = jnp.stack([low.astype(jnp.int32), part.astype(jnp.int32), (place == 0).astype(jnp.int32)])
    smem = pl.BlockSpec(memory_space=pltpu.SMEM)
    bf = jnp.bfloat16
    sel_send = jnp.asarray(pick_send, bf)
    flip = [(p, groups - 1 - p) for p in range(groups)]
    sends, mine, other = [], [], []
    for d in range(depth):
        send = pl.pallas_call(
            pick_kernel,
            grid_spec=pltpu.PrefetchScalarGridSpec(
                num_scalar_prefetch=1,
                grid=(1,),
                in_specs=[whole(kept, rows),
                          pl.BlockSpec((1, 1, rows, length), lambda i, where, d=d: (where[0], d, 0, 0))],
                out_specs=near,
            ),
            out_shape=pltpu.VMEM((kept, length), f32),
            name="pick",
        )(part.astype(jnp.int32).reshape(1), sel_send, psf_spectra)
        sends.append(send)
        mine.append(lax.ppermute(send, "row", flip))
    late, early, _ = lax.optimization_barrier((psf_spectra, volume, sends[-1]))
    edge = late[:, :, 0, :].astype(f32).reshape(2 * depth, length)
    edge = jnp.pad(edge, ((0, pair - 2 * depth), (0, 0)))
    ends = [(groups - p, p) for p in range(1, groups // 2)] + [(groups // 2, 0)]
    edge = lax.ppermute(edge, "row", ends)
    for d in range(depth):
        other.append(lax.ppermute(mine[d], "vol", [(0, 1), (1, 0)]))

    scale = 0.5 / (length * length)
    many_t = 2
    width = many_t * lanes

    def mix_kernel(where_ref, own_l_ref, own_h_ref, psf_ref, edge_ref, *rest):
        mine_refs, other_refs = rest[:depth], rest[depth:2 * depth]
        a_ref, b_ref, o_s, p_s, e_s = rest[2 * depth:]
        step = pl.program_id(0)

        @pl.when(step == 0)
        def _():
            zero = where_ref[2] == 1
            is_low = where_ref[0] == 1
            sel = jnp.where(is_low, own_l_ref[...], own_h_ref[...]).astype(bf)
            first = lax.broadcasted_iota(jnp.int32, (SUB, length), 0) == 0
            for c in range(2):
                mine_here = where_ref[1] == c
                for d in range(depth):
                    row = c * depth + d
                    base = row * kept
                    kept_own = mm(sel, psf_ref[c, d], NN)
                    o_s[base:base + kept, :] = kept_own.astype(bf)
                    p = jnp.where(mine_here, mine_refs[d][...], other_refs[d][...])
                    swap = jnp.where(zero, kept_own[0:1, :], edge_ref[row:row + 1, :])
                    head = jnp.where(jnp.logical_and(first, is_low), swap, p[:SUB])
                    p_s[base:base + kept, :] = jnp.concatenate([head, p[SUB:]], 0).astype(bf)
            e_s[...] = edge_ref[...].astype(bf)

        freq = lax.broadcasted_iota(jnp.int32, (length, width), 0)
        col = lax.broadcasted_iota(jnp.int32, (length, width), 1)
        target = (col % lanes) * groups + step * many_t + col // lanes
        hot = jnp.where(freq == target, 1.0, 0.0).astype(bf)
        hot_rev = jnp.where(freq == (length - target) % length, 1.0, 0.0).astype(bf)
        plain = mm(o_s[...], hot, NN)
        mirror = mm(p_s[...], hot_rev, NN)
        e_plain = mm(e_s[...], hot, NN)
        e_mirror = mm(e_s[...], hot_rev, NN)
        zero = jnp.where(where_ref[2] == 1, 1.0, 0.0).astype(f32)
        b_ref[...] = jnp.zeros((2, SUB, width), f32)
        first = lax.broadcasted_iota(jnp.int32, (SUB, width), 0) == 0
        for c in range(2):
            sign = 1.0 if c == 0 else -1.0
            for d in range(depth):
                row = c * depth + d
                base = row * kept
                h = (plain[base:base + kept] + sign * mirror[base:base + kept]) * scale
                e = (e_plain[row:row + 1] + sign * e_mirror[row:row + 1]) * scale
                a0 = h[:SUB] * (1.0 - 0.75 * zero) + (0.25 * zero) * e
                b0 = (h[:SUB] - e) * (0.25 * zero)
                a_ref[c, d, :SUB, :] = jnp.where(first, a0, h[:SUB])
                a_ref[c, d, SUB:, :] = h[SUB:]
                b_ref[c, d:d + 1, :] = b0[0:1, :]

    planes = 2 * depth * kept
    a_all, b_all = pl.pallas_call(
        mix_kernel,
        grid=(groups // many_t,),
        in_specs=[smem, whole(kept, rows), whole(kept, rows), whole(2, depth, rows, length),
                  whole(pair, length)] + [whole(kept, length)] * (2 * depth),
        out_specs=[pl.BlockSpec((2, depth, kept, width), lambda i: (0, 0, 0, i)),
                   pl.BlockSpec((2, SUB, width), lambda i: (0, 0, i))],
        out_shape=[jax.ShapeDtypeStruct((2, depth, kept, length), f32),
                   jax.ShapeDtypeStruct((2, SUB, length), f32)],
        scratch_shapes=[pltpu.VMEM((planes, length), bf), pltpu.VMEM((planes, length), bf),
                        pltpu.VMEM((pair, length), bf)],
        name="mix",
    )(flags, jnp.asarray(pick_own), jnp.asarray(pick_high), psf_spectra, edge, *mine, *other)

    def forward_kernel(wy_ref, w0_ref, turn_ref, v_ref, o_ref, z):
        def read(i, a):
            return v_ref[0, pl.ds(pl.multiple_of(i * SUB, SUB), SUB), a * lanes:(a + 1) * lanes]

        def emit(t, out):
            o_ref[:, 0, t] = out.reshape(groups, 2, SUB, rows)

        y_forward(read, emit, z, wy_ref, w0_ref, turn_ref, groups, rows, lanes)

    outgoing = pl.pallas_call(
        forward_kernel,
        grid=(depth,),
        in_specs=y_specs + [pl.BlockSpec((1, rows, length), lambda d: (d, 0, 0))],
        out_specs=pl.BlockSpec((groups, 1, tiles, 2, SUB, lanes), lambda d: (0, d, 0, 0, 0, 0)),
        out_shape=jax.ShapeDtypeStruct(many(depth), f32),
        scratch_shapes=[y_scratch],
        name="forward_y",
    )(*y_tables, early)

    def swap(field):
        return lax.all_to_all(field, "row", split_axis=0, concat_axis=0, tiled=True)

    outgoing, _ = lax.optimization_barrier((outgoing, mine[0]))
    arrived = swap(outgoing)

    block = groups * pair

    small = groups * SUB
    lead = lambda: lax.broadcasted_iota(jnp.int32, (SUB, lanes), 0)

    steps = tiles // 2

    def per_step(n, count):
        return pltpu.VMEM((count, n * block, 2 * lanes), f32)

    def project_kernel(wx_any, wxi_any, turn_ref, s_ref, a_any, b_any, o_ref,
                       wx_ref, wxi_ref, a_s, b_ref, z_s, t_all, zc_s, sems):
        loads = [pltpu.make_async_copy(wx_any, wx_ref, sems.at[0])]
        for step in range(steps):
            mine_rows = pl.ds(step * pair, pair)
            loads.append(pltpu.make_async_copy(a_any.at[:, :, mine_rows, :], a_s.at[step], sems.at[step + 1]))
        loads.append(pltpu.make_async_copy(b_any, b_ref, sems.at[steps + 1]))
        loads.append(pltpu.make_async_copy(wxi_any, wxi_ref, sems.at[steps + 2]))
        for n in (0, 1, steps + 1, steps + 2, *range(2, steps + 1)):
            loads[n].start()

        def forward(step):
            z, zc, t_s = z_s.at[step], zc_s.at[step], t_all.at[step]
            for d in range(depth):
                for h in range(2):
                    j = step * 2 + h
                    tile = [(s_ref[s, d, j, 0], s_ref[s, d, j, 1]) for s in range(groups)]
                    x_radix(tile, z, d * block + h * SUB, turn_ref, lanes, pair)
                if step == 0 and d == 0:
                    loads[0].wait()
                zc[d * block:(d + 1) * block, :] = data_table(z[d * block:(d + 1) * block, :], wx_ref)
            loads[step + 1].wait()
            for t in range(groups):
                here = slice(t * pair, (t + 1) * pair)
                cols = slice(t * lanes, (t + 1) * lanes)
                re = im = None
                for d in range(depth):
                    at = slice(d * block + t * pair, d * block + (t + 1) * pair)
                    zr, zi = zc[at, :lanes], zc[at, lanes:]
                    kr, ki = a_s[step, 0, d, :, cols], a_s[step, 1, d, :, cols]
                    re = plus(re, zr * kr - zi * ki)
                    im = plus(im, zr * ki + zi * kr)
                t_s[here, :lanes] = re
                t_s[here, lanes:] = im

        def packed():
            z, zc, t_s = z_s.at[steps], zc_s.at[steps], t_all.at[0]

            def row(s, c):
                out = s_ref[s, 0, 0, c, 0:1, :]
                for d in range(1, depth):
                    out = jnp.where(lead() == d, s_ref[s, d, 0, c, 0:1, :], out)
                return jnp.broadcast_to(out, (SUB, lanes))

            x_radix([(row(s, 0), -row(s, 1)) for s in range(groups)], z, 0, turn_ref, lanes, SUB)
            zc[:small, :] = data_table(z[:small, :], wx_ref)
            loads[steps + 1].wait()
            for t in range(groups):
                at = slice(t * SUB, (t + 1) * SUB)
                cols = slice(t * lanes, (t + 1) * lanes)
                zr, zi = zc[at, :lanes], zc[at, lanes:]
                kr, ki = b_ref[0, :, cols], b_ref[1, :, cols]
                top = slice(t * pair, t * pair + 1)
                t_s[top, :lanes] += jnp.sum(zr * kr - zi * ki, axis=0, keepdims=True)
                t_s[top, lanes:] += jnp.sum(zr * ki + zi * kr, axis=0, keepdims=True)

        def back(step):
            zc = z_s.at[step]
            zc[:block, :] = data_table(t_all[step], wxi_ref)
            for h in range(2):
                for s, (re, im) in enumerate(x_unradix(zc, h * SUB, turn_ref, groups, lanes, pair)):
                    o_ref[s, step * 2 + h, 0] = re
                    o_ref[s, step * 2 + h, 1] = im

        for step in range(steps):
            forward(step)
            if step == 0:
                packed()
                loads[steps + 2].wait()
            back(step)

    hbm = pl.BlockSpec(memory_space=pl.ANY)
    outgoing = pl.pallas_call(
        project_kernel,
        in_specs=[hbm, hbm, whole(*turn.shape), near, hbm, hbm],
        out_specs=near,
        out_shape=pltpu.VMEM(send_shape, f32),
        scratch_shapes=[pltpu.VMEM(w_x.shape, bf), pltpu.VMEM(w_xi.shape, bf),
                        pltpu.VMEM((steps, 2, depth, pair, length), f32), pltpu.VMEM((2, SUB, length), f32),
                        per_step(depth, steps + 1), per_step(1, steps), per_step(depth, steps + 1),
                        pltpu.SemaphoreType.DMA((steps + 3,))],
        compiler_params=pltpu.CompilerParams(vmem_limit_bytes=36 << 20),
        name="project_x",
    )(far(w_x), far(w_xi), turn, keep(arrived), far(a_all), far(b_all))
    arrived = swap(outgoing)

    def ratio_kernel(wy_ref, w0_ref, turn_ref, g_ref, bg_ref, me_ref, p_ref, o_ref, z):
        def fetch(t):
            return g_ref[:, t].reshape(groups * 2 * SUB, rows)

        def write(here, outs):
            ratio = []
            for a, value in enumerate(outs):
                cols = slice(a * lanes, (a + 1) * lanes)
                p_ref[here, cols] = value
                ratio.append(me_ref[here, cols] / jnp.maximum(value + bg_ref[here, cols], FLOOR))
            y_store(ratio, z, here, turn_ref, groups, lanes)

        y_inverse(fetch, write, z, wy_ref, w0_ref, turn_ref, groups, rows, lanes)
        for t in range(tiles):
            out = table_data(w0_ref if t == 0 else wy_ref, z[t])
            o_ref[:, t] = out.reshape(groups, 2, SUB, rows)

    projection, outgoing = pl.pallas_call(
        ratio_kernel,
        in_specs=[near] * 6,
        out_specs=[whole(rows, length), near],
        out_shape=[jax.ShapeDtypeStruct((rows, length), f32), pltpu.VMEM(send_shape, f32)],
        scratch_shapes=[y_scratch],
        compiler_params=pltpu.CompilerParams(vmem_limit_bytes=16 << 20),
        name="ratio",
    )(*y_near, keep(arrived), keep(background), keep(measured))
    arrived = swap(outgoing)

    def correct_kernel(wx_ref, wxi_ref, turn_ref, s_ref, a_ref, b_ref, o_ref, z_s, zq_s, zc_s, cs_s):
        def forward(step):
            z, zq, c_s = z_s.at[step], zq_s.at[step], cs_s.at[step]
            for h in range(2):
                j = step * 2 + h
                tile = [(s_ref[s, j, 0], s_ref[s, j, 1]) for s in range(groups)]
                x_radix(tile, z, h * SUB, turn_ref, lanes, pair)
            zq[...] = data_table(z[...], wx_ref)
            mine_rows = slice(step * pair, (step + 1) * pair)
            for t in range(groups):
                here = slice(t * pair, (t + 1) * pair)
                cols = slice(t * lanes, (t + 1) * lanes)
                zr, zi = zq[here, :lanes], zq[here, lanes:]
                for d in range(depth):
                    at = slice(d * block + t * pair, d * block + (t + 1) * pair)
                    kr, ki = a_ref[0, d, mine_rows, cols], a_ref[1, d, mine_rows, cols]
                    c_s[at, :lanes] = zr * kr + zi * ki
                    c_s[at, lanes:] = zi * kr - zr * ki

        def packed():
            z, zq, c_s = z_s.at[steps], zq_s.at[steps], cs_s.at[0]
            tile = [(s_ref[s, 0, 0], -s_ref[s, 0, 1]) for s in range(groups)]
            x_radix(tile, z, 0, turn_ref, lanes, SUB)
            zq[:small, :] = data_table(z[:small, :], wx_ref)
            for t in range(groups):
                at = slice(t * SUB, t * SUB + 1)
                cols = slice(t * lanes, (t + 1) * lanes)
                zr, zi = zq[at, :lanes], zq[at, lanes:]
                kr, ki = b_ref[0, :, cols], b_ref[1, :, cols]
                re, im = zr * kr + zi * ki, zi * kr - zr * ki
                for d in range(depth):
                    top = slice(d * block + t * pair, d * block + t * pair + 1)
                    c_s[top, :lanes] += re[d:d + 1, :]
                    c_s[top, lanes:] += im[d:d + 1, :]

        def back(step):
            zc, c_s = zc_s.at[step], cs_s.at[step]
            for d in range(depth):
                zc[d * block:(d + 1) * block, :] = data_table(c_s[d * block:(d + 1) * block, :], wxi_ref)
                for h in range(2):
                    out = x_unradix(zc, d * block + h * SUB, turn_ref, groups, lanes, pair)
                    for s, (re, im) in enumerate(out):
                        o_ref[s, d, step * 2 + h, 0] = re
                        o_ref[s, d, step * 2 + h, 1] = im

        for step in range(steps):
            forward(step)
            if step == 0:
                packed()
            back(step)

    outgoing = pl.pallas_call(
        correct_kernel,
        in_specs=[near] * 6,
        out_specs=near,
        out_shape=pltpu.VMEM(many(depth), f32),
        scratch_shapes=[per_step(1, steps + 1), per_step(1, steps + 1), per_step(depth, steps), per_step(depth, steps)],
        compiler_params=pltpu.CompilerParams(vmem_limit_bytes=32 << 20),
        name="correct_x",
    )(*x_near, keep(arrived), keep(a_all), keep(b_all))
    arrived = swap(outgoing)

    def final_kernel(wy_ref, w0_ref, turn_ref, g_ref, v_ref, o_ref, z, out_s, sems):
        def products(d):
            for t in range(tiles):
                spectrum = g_ref[:, d, t].reshape(groups * 2 * SUB, rows)
                z[d % 2, t] = data_table(spectrum.T, w0_ref if t == 0 else wy_ref)

        def lines(d, first, last):
            for i in range(first, last):
                here = slice(i * SUB, (i + 1) * SUB)
                for a, value in enumerate(c2r(y_load(z.at[d % 2], here, turn_ref, groups, lanes))):
                    cols = slice(a * lanes, (a + 1) * lanes)
                    out_s[d, here, cols] = v_ref[d, here, cols] * value

        copies = []
        products(0)
        for d in range(depth):
            if d + 1 < depth:
                products(d + 1)
            lines(d, 0, rows // SUB)
            copies.append(pltpu.make_async_copy(out_s.at[d], o_ref.at[d], sems.at[d]))
            copies[d].start()
        for copy in copies:
            copy.wait()

    new_volume = pl.pallas_call(
        final_kernel,
        in_specs=[near] * 5,
        out_specs=pl.BlockSpec(memory_space=pl.ANY),
        out_shape=pltpu.HBM((depth, rows, length), f32),
        scratch_shapes=[pltpu.VMEM((2, tiles, rows, 2 * lanes), f32),
                        pltpu.VMEM((depth, rows, length), f32), pltpu.SemaphoreType.DMA((depth,))],
        compiler_params=pltpu.CompilerParams(vmem_limit_bytes=16 << 20),
        name="final_y",
    )(*y_near, keep(arrived), keep(volume))
    return new_volume, projection


def solution(mesh):
    groups, parts = mesh.shape["row"], mesh.shape["vol"]

    def shards(volume, psf_spectra, background, measured):
        rows = volume.shape[1]
        fits = parts == 2 and rows == LANES and rows == SUB * groups
        body = fast_shards if fits else generic_shards
        return body(volume, psf_spectra, background, measured)

    in_specs = (
        P("vol", "row", None),
        P(None, None, "row", None),
        P("row", None),
        P(("vol", "row"), None),
    )
    out_specs = (P("vol", "row", None), P(("vol", "row"), None))
    return jax.shard_map(shards, mesh=mesh, in_specs=in_specs, out_specs=out_specs, check_vma=False)
```

```python
import math

import jax
import jax.numpy as jnp
import numpy as np
from jax import lax
from jax.experimental import pallas as pl
from jax.experimental.pallas import tpu as pltpu
from jax.sharding import PartitionSpec as P


FLOOR = 0.5
HIGHEST = lax.Precision.HIGHEST
LANES = 128
SUB = 8


def phase_pair(first_extent, second_extent, modulus, direction):
    first_idx = jnp.arange(first_extent, dtype=jnp.int32)
    second_idx = jnp.arange(second_extent, dtype=jnp.int32)
    phases = first_idx[:, None] * second_idx[None, :] % modulus
    angles = phases.astype(jnp.float32) * (2.0 * math.pi / modulus)
    return (jnp.cos(angles), direction * jnp.sin(angles))


def contract(pattern, fields, coeffs, real_only):
    real_part, imag_part = fields
    coeff_real, coeff_imag = coeffs

    def product(operand, table_side):
        return jnp.einsum(pattern, operand, table_side, precision=HIGHEST)

    if imag_part is None:
        return (product(real_part, coeff_real), product(real_part, coeff_imag))
    out_real = product(real_part, coeff_real) - product(imag_part, coeff_imag)
    if real_only:
        return (out_real, None)
    return (out_real, product(real_part, coeff_imag) + product(imag_part, coeff_real))


def rotate(fields, factors):
    real_part, imag_part = fields
    factor_real, factor_imag = factors
    return (
        real_part * factor_real - imag_part * factor_imag,
        real_part * factor_imag + imag_part * factor_real,
    )


def leading_pass(fields, groups, direction):
    batch_size, row_count, length = fields[0].shape
    inner_count = length // groups
    shaped = tuple(
        None if member is None else member.reshape(batch_size, row_count, inner_count, groups)
        for member in fields
    )
    sectioned = contract(
        "bqnm,nk->bqkm", shaped, phase_pair(inner_count, inner_count, inner_count, direction), False
    )
    sectioned = rotate(sectioned, phase_pair(inner_count, groups, length, direction))
    sectioned = contract(
        "bqkm,mp->bpkq", sectioned, phase_pair(groups, groups, groups, direction), False
    )
    return tuple(member.reshape(batch_size, groups, inner_count * row_count) for member in sectioned)


def trailing_pass(fields, row_count, direction, real_only):
    batch_size, groups, merged = fields[0].shape
    inner_count = merged // row_count
    length = groups * row_count
    shaped = tuple(member.reshape(batch_size, groups, inner_count, row_count) for member in fields)
    sectioned = contract(
        "bskq,st->bktq", shaped, phase_pair(groups, groups, groups, direction), False
    )
    sectioned = rotate(sectioned, phase_pair(groups, row_count, length, direction))
    sectioned = contract(
        "bktq,qu->bkut", sectioned, phase_pair(row_count, row_count, row_count, direction), real_only
    )
    return tuple(
        None if member is None else member.reshape(batch_size, inner_count, length)
        for member in sectioned
    )


def generic_shards(volume, psf_spectra, background, measured):
    groups = lax.axis_size("row")
    row_count = volume.shape[1]
    length = volume.shape[2]
    inverse_scale = 1.0 / (length * length)
    response_real = psf_spectra[0].astype(jnp.float32)
    response_imag = psf_spectra[1].astype(jnp.float32)

    def swap(field):
        return lax.all_to_all(field, "row", split_axis=1, concat_axis=1, tiled=True)

    outgoing = leading_pass((volume, None), groups, -1.0)
    spec_real, spec_imag = trailing_pass(
        (swap(outgoing[0]), swap(outgoing[1])), row_count, -1.0, False
    )
    prod_real = spec_real * response_real - spec_imag * response_imag
    prod_imag = spec_real * response_imag + spec_imag * response_real
    summed = (jnp.sum(prod_real, axis=0, keepdims=True), jnp.sum(prod_imag, axis=0, keepdims=True))
    outgoing = leading_pass(summed, groups, 1.0)
    arrived = (swap(outgoing[0]), swap(outgoing[1]))
    projection = trailing_pass(arrived, row_count, 1.0, True)[0][0] * inverse_scale
    quotient = measured / jnp.maximum(projection + background, FLOOR)
    outgoing = leading_pass((quotient[None], None), groups, -1.0)
    arrived = (swap(outgoing[0]), swap(outgoing[1]))
    ratio_real, ratio_imag = trailing_pass(arrived, row_count, -1.0, False)
    corr_real = ratio_real * response_real + ratio_imag * response_imag
    corr_imag = ratio_imag * response_real - ratio_real * response_imag
    outgoing = leading_pass((corr_real, corr_imag), groups, 1.0)
    arrived = (swap(outgoing[0]), swap(outgoing[1]))
    correction = trailing_pass(arrived, row_count, 1.0, True)[0] * inverse_scale
    return (volume * correction, projection)


def times(z, angle):
    re, im = z
    c, s = math.cos(angle), math.sin(angle)
    if abs(s) < 1e-12:
        return z if c > 0 else (-re, None if im is None else -im)
    if abs(c) < 1e-12:
        if im is None:
            return (None, re if s > 0 else -re)
        return (-im, re) if s > 0 else (im, -re)
    if im is None:
        return (re * c, re * s)
    if abs(abs(c) - abs(s)) < 1e-12:
        sc, ss = math.copysign(1.0, c), math.copysign(1.0, s)
        a = re if sc > 0 else -re
        b = im if sc > 0 else -im
        r, i = (a - im, b + re) if ss > 0 else (a + im, b - re)
        return (r * abs(c), i * abs(c))
    return (re * c - im * s, re * s + im * c)


def plus(a, b):
    if a is None:
        return b
    return a if b is None else a + b


def minus(a, b):
    if b is None:
        return a
    return -b if a is None else a - b


def cadd(a, b):
    return (plus(a[0], b[0]), plus(a[1], b[1]))


def csub(a, b):
    return (minus(a[0], b[0]), minus(a[1], b[1]))


def conj(a):
    return (a[0], None if a[1] is None else -a[1])


def cfft(xs, sign):
    n = len(xs)
    if n == 1:
        return list(xs)
    even, odd = cfft(xs[0::2], sign), cfft(xs[1::2], sign)
    turned = [times(odd[t], sign * 2.0 * math.pi * t / n) for t in range(n // 2)]
    return [cadd(even[t], turned[t]) for t in range(n // 2)] + [
        csub(even[t], turned[t]) for t in range(n // 2)
    ]


def rfft(xs):
    n = len(xs)
    if n == 2:
        return [(xs[0] + xs[1], None), (xs[0] - xs[1], None)]
    even, odd = rfft(xs[0::2]), rfft(xs[1::2])
    out = [None] * (n // 2 + 1)
    for t in range(n // 4 + 1):
        turned = times(odd[t], -2.0 * math.pi * t / n)
        out[t] = cadd(even[t], turned)
        if t < n // 4:
            out[n // 2 - t] = conj(csub(even[t], turned))
    return out


def c2r(zs):
    n = 2 * (len(zs) - 1)
    if n == 2:
        return [zs[0][0] + zs[1][0], zs[0][0] - zs[1][0]]
    q = n // 4
    even, odd = [], []
    for t in range(q):
        mirror = conj(zs[n // 2 - t])
        even.append(cadd(zs[t], mirror))
        odd.append(times(csub(zs[t], mirror), 2.0 * math.pi * t / n))
    even.append((zs[q][0] * 2.0, None))
    odd.append((zs[q][1] * -2.0, None))
    a, b = c2r(even), c2r(odd)
    return [half[i] for i in range(n // 2) for half in (a, b)]


def split_table(table):
    high = table.astype(jnp.bfloat16)
    low = (table - high.astype(np.float64)).astype(jnp.bfloat16)
    return np.stack([high, low])


def make_tables(groups, lanes):
    length = groups * lanes
    per = lanes // groups
    pos = np.arange(lanes)
    w_y = np.zeros((groups, 2, SUB, 2, lanes))
    w_0 = np.zeros((groups, 2, SUB, 2, lanes))
    half = SUB // 2
    for p in range(groups):
        for r in range(SUB):
            ang = 2.0 * np.pi * ((per * p + r) * pos % lanes) / lanes
            w_y[p, 0, r] = np.cos(ang), np.sin(ang)
            w_y[p, 1, r] = -np.sin(ang), np.cos(ang)
            if r < half:
                unit = per * p + r
                if r == 0 and p >= groups // 2:
                    unit = per * p + per // 2
                ang = 2.0 * np.pi * (groups * unit * pos % length) / length
                w_0[p, 0, r, 0] = np.cos(ang)
                w_0[p, 1, r, 0] = -np.sin(ang)
                if r == 0 and p == 0:
                    w_0[p, 1, r, 0] = (-1.0) ** pos
            else:
                ang = (groups * (per * p + r - half) + groups // 2) * pos % length
                ang = 2.0 * np.pi * ang / length
                w_0[p, 0, r, 1] = np.cos(ang)
                w_0[p, 1, r, 1] = -np.sin(ang)
    rows = groups * 2 * SUB
    ang = 2.0 * np.pi * (pos[:, None] * pos[None, :] % lanes) / lanes
    w_x = np.block([[np.cos(ang), -np.sin(ang)], [np.sin(ang), np.cos(ang)]])
    ang = 2.0 * np.pi * (np.arange(groups)[:, None] * pos[None, :] % length) / length
    turn = np.stack([np.cos(ang), -np.sin(ang)], axis=1).astype(np.float32)
    w_y, w_0 = split_table(w_y.reshape(rows, 2 * lanes)), split_table(w_0.reshape(rows, 2 * lanes))
    return w_y, w_0, split_table(w_x), split_table(w_x.T), turn


def kept_rows(groups, lanes):
    per = lanes // groups
    half = SUB // 2
    own = [groups * w for w in range(half)] + [groups * w + groups // 2 for w in range(half)]
    for tile in range(1, groups // 2):
        own += [groups * w + tile for w in range(per)]
    return own


NN = (((1,), (0,)), ((), ()))
NT = (((1,), (1,)), ((), ()))


def halves(x):
    high = x.astype(jnp.bfloat16)
    return high, (x - high.astype(jnp.float32)).astype(jnp.bfloat16)


def mm(a, b, dims):
    return lax.dot_general(a, b, dims, preferred_element_type=jnp.float32)


def data_table(x, table):
    high, low = halves(x)
    return mm(high, table[0], NN) + (mm(low, table[0], NN) + mm(high, table[1], NN))


def table_data(table, x):
    high, low = halves(x)
    return mm(table[0], high, NT) + (mm(table[0], low, NT) + mm(table[1], high, NT))


def y_store(xs, z, here, turn, groups, lanes):
    out = rfft(xs)
    z[0, here, :lanes] = out[0][0]
    z[0, here, lanes:] = out[groups // 2][0]
    for t in range(1, groups // 2):
        re, im = out[t]
        c, s = turn[t, 0:1, :], turn[t, 1:2, :]
        z[t, here, :lanes] = re * c - im * s
        z[t, here, lanes:] = re * s + im * c


def y_forward(read, emit, z, w_y, w_0, turn, groups, rows, lanes):
    def chunk(i, carry):
        here = pl.ds(pl.multiple_of(i * SUB, SUB), SUB)
        y_store([read(i, a) for a in range(groups)], z, here, turn, groups, lanes)
        return carry

    lax.fori_loop(0, rows // SUB, chunk, 0)
    for t in range(groups // 2):
        emit(t, table_data(w_0 if t == 0 else w_y, z[t]))


def y_load(z, here, turn, groups, lanes):
    zs = [(z[0, here, :lanes] * 2.0, None)]
    for t in range(1, groups // 2):
        re, im = z[t, here, :lanes], z[t, here, lanes:]
        c, s = turn[t, 0:1, :], turn[t, 1:2, :]
        zs.append((re * c + im * s, im * c - re * s))
    zs.append((z[0, here, lanes:] * 2.0, None))
    return zs


def y_inverse(fetch, write, z, w_y, w_0, turn, groups, rows, lanes):
    for t in range(groups // 2):
        z[t] = data_table(fetch(t).T, w_0 if t == 0 else w_y)
    for i in range(rows // SUB):
        here = slice(i * SUB, (i + 1) * SUB)
        write(here, c2r(y_load(z, here, turn, groups, lanes)))


def x_radix(tile, z, base, turn, lanes, step):
    for t, (re, im) in enumerate(cfft(tile, -1.0)):
        here = slice(base + t * step, base + t * step + SUB)
        if t == 0:
            z[here, :lanes] = re
            z[here, lanes:] = im
        else:
            c, s = turn[t, 0:1, :], turn[t, 1:2, :]
            z[here, :lanes] = re * c - im * s
            z[here, lanes:] = re * s + im * c


def x_unradix(z, base, turn, groups, lanes, step):
    zs = []
    for t in range(groups):
        here = slice(base + t * step, base + t * step + SUB)
        re, im = z[here, :lanes], z[here, lanes:]
        if t:
            c, s = turn[t, 0:1, :], turn[t, 1:2, :]
            re, im = re * c + im * s, im * c - re * s
        zs.append((re, im))
    return cfft(zs, 1.0)


def fast_shards(volume, psf_spectra, background, measured):
    groups = lax.axis_size("row")
    depth, rows, length = volume.shape
    lanes = LANES
    tiles = groups // 2
    kept = tiles * SUB
    pair = 2 * SUB
    f32 = jnp.float32
    place = lax.axis_index("row")
    part = lax.axis_index("vol")
    w_y, w_0, w_x, w_xi, turn = (jnp.asarray(t) for t in make_tables(groups, lanes))
    own_rows = kept_rows(groups, rows)

    whole = lambda *shape: pl.BlockSpec(shape, lambda *_: (0,) * len(shape))
    near = pl.BlockSpec(memory_space=pltpu.VMEM)

    def keep(x):
        return pltpu.with_memory_space_constraint(x, pltpu.VMEM)

    def far(x):
        return pltpu.with_memory_space_constraint(x, pltpu.HBM)

    y_tables, x_tables = (w_y, w_0, turn), (w_x, w_xi, turn)
    y_near = tuple(keep(t) for t in (w_y, w_0, turn))
    x_near = tuple(keep(t) for t in x_tables)
    y_specs = [whole(*t.shape) for t in y_tables]
    x_specs = [whole(*t.shape) for t in x_tables]
    y_scratch = pltpu.VMEM((tiles, rows, 2 * lanes), f32)
    send_shape = (groups, tiles, 2, SUB, lanes)

    def many(n):
        return (groups, n, tiles, 2, SUB, lanes)

    low = place < groups // 2
    mid = rows // 2
    pick_send = np.zeros((kept, rows), np.float32)
    pick_own = np.zeros((kept, rows), np.float32)
    for r, k in enumerate(own_rows):
        pick_send[r, (rows - k) if k else mid] = 1.0
        pick_own[r, k] = 1.0
    pick_high = pick_own.copy()
    pick_high[0] = 0.0
    pick_high[0, mid] = 1.0

    def pick_kernel(part_ref, sel_ref, psf_ref, send_ref):
        send_ref[...] = mm(sel_ref[...], psf_ref[0, 0], NN)

    flags = jnp.stack([low.astype(jnp.int32), part.astype(jnp.int32), (place == 0).astype(jnp.int32)])
    smem = pl.BlockSpec(memory_space=pltpu.SMEM)
    bf = jnp.bfloat16
    sel_send = jnp.asarray(pick_send, bf)
    flip = [(p, groups - 1 - p) for p in range(groups)]
    sends, mine, other = [], [], []
    for d in range(depth):
        send = pl.pallas_call(
            pick_kernel,
            grid_spec=pltpu.PrefetchScalarGridSpec(
                num_scalar_prefetch=1,
                grid=(1,),
                in_specs=[whole(kept, rows),
                          pl.BlockSpec((1, 1, rows, length), lambda i, where, d=d: (where[0], d, 0, 0))],
                out_specs=near,
            ),
            out_shape=pltpu.VMEM((kept, length), f32),
            name="pick",
        )(part.astype(jnp.int32).reshape(1), sel_send, psf_spectra)
        sends.append(send)
        mine.append(lax.ppermute(send, "row", flip))
    late, early, _ = lax.optimization_barrier((psf_spectra, volume, sends[-1]))
    edge = late[:, :, 0, :].astype(f32).reshape(2 * depth, length)
    edge = jnp.pad(edge, ((0, pair - 2 * depth), (0, 0)))
    ends = [(groups - p, p) for p in range(1, groups // 2)] + [(groups // 2, 0)]
    edge = lax.ppermute(edge, "row", ends)
    for d in range(depth):
        other.append(lax.ppermute(mine[d], "vol", [(0, 1), (1, 0)]))

    scale = 0.5 / (length * length)
    many_t = 2
    width = many_t * lanes

    def mix_kernel(where_ref, own_l_ref, own_h_ref, psf_ref, edge_ref, *rest):
        mine_refs, other_refs = rest[:depth], rest[depth:2 * depth]
        a_ref, b_ref, o_s, p_s, e_s = rest[2 * depth:]
        step = pl.program_id(0)

        @pl.when(step == 0)
        def _():
            zero = where_ref[2] == 1
            is_low = where_ref[0] == 1
            sel = jnp.where(is_low, own_l_ref[...], own_h_ref[...]).astype(bf)
            first = lax.broadcasted_iota(jnp.int32, (SUB, length), 0) == 0
            for c in range(2):
                mine_here = where_ref[1] == c
                for d in range(depth):
                    row = c * depth + d
                    base = row * kept
                    kept_own = mm(sel, psf_ref[c, d], NN)
                    o_s[base:base + kept, :] = kept_own.astype(bf)
                    p = jnp.where(mine_here, mine_refs[d][...], other_refs[d][...])
                    swap = jnp.where(zero, kept_own[0:1, :], edge_ref[row:row + 1, :])
                    head = jnp.where(jnp.logical_and(first, is_low), swap, p[:SUB])
                    p_s[base:base + kept, :] = jnp.concatenate([head, p[SUB:]], 0).astype(bf)
            e_s[...] = edge_ref[...].astype(bf)

        freq = lax.broadcasted_iota(jnp.int32, (length, width), 0)
        col = lax.broadcasted_iota(jnp.int32, (length, width), 1)
        target = (col % lanes) * groups + step * many_t + col // lanes
        hot = jnp.where(freq == target, 1.0, 0.0).astype(bf)
        hot_rev = jnp.where(freq == (length - target) % length, 1.0, 0.0).astype(bf)
        plain = mm(o_s[...], hot, NN)
        mirror = mm(p_s[...], hot_rev, NN)
        e_plain = mm(e_s[...], hot, NN)
        e_mirror = mm(e_s[...], hot_rev, NN)
        zero = jnp.where(where_ref[2] == 1, 1.0, 0.0).astype(f32)
        b_ref[...] = jnp.zeros((2, SUB, width), f32)
        first = lax.broadcasted_iota(jnp.int32, (SUB, width), 0) == 0
        for c in range(2):
            sign = 1.0 if c == 0 else -1.0
            for d in range(depth):
                row = c * depth + d
                base = row * kept
                h = (plain[base:base + kept] + sign * mirror[base:base + kept]) * scale
                e = (e_plain[row:row + 1] + sign * e_mirror[row:row + 1]) * scale
                a0 = h[:SUB] * (1.0 - 0.75 * zero) + (0.25 * zero) * e
                b0 = (h[:SUB] - e) * (0.25 * zero)
                a_ref[c, d, :SUB, :] = jnp.where(first, a0, h[:SUB])
                a_ref[c, d, SUB:, :] = h[SUB:]
                b_ref[c, d:d + 1, :] = b0[0:1, :]

    planes = 2 * depth * kept
    a_all, b_all = pl.pallas_call(
        mix_kernel,
        grid=(groups // many_t,),
        in_specs=[smem, whole(kept, rows), whole(kept, rows), whole(2, depth, rows, length),
                  whole(pair, length)] + [whole(kept, length)] * (2 * depth),
        out_specs=[pl.BlockSpec((2, depth, kept, width), lambda i: (0, 0, 0, i)),
                   pl.BlockSpec((2, SUB, width), lambda i: (0, 0, i))],
        out_shape=[jax.ShapeDtypeStruct((2, depth, kept, length), f32),
                   jax.ShapeDtypeStruct((2, SUB, length), f32)],
        scratch_shapes=[pltpu.VMEM((planes, length), bf), pltpu.VMEM((planes, length), bf),
                        pltpu.VMEM((pair, length), bf)],
        name="mix",
    )(flags, jnp.asarray(pick_own), jnp.asarray(pick_high), psf_spectra, edge, *mine, *other)

    def forward_kernel(wy_ref, w0_ref, turn_ref, v_ref, o_ref, z):
        def read(i, a):
            return v_ref[0, pl.ds(pl.multiple_of(i * SUB, SUB), SUB), a * lanes:(a + 1) * lanes]

        def emit(t, out):
            o_ref[:, 0, t] = out.reshape(groups, 2, SUB, rows)

        y_forward(read, emit, z, wy_ref, w0_ref, turn_ref, groups, rows, lanes)

    outgoing = pl.pallas_call(
        forward_kernel,
        grid=(depth,),
        in_specs=y_specs + [pl.BlockSpec((1, rows, length), lambda d: (d, 0, 0))],
        out_specs=pl.BlockSpec((groups, 1, tiles, 2, SUB, lanes), lambda d: (0, d, 0, 0, 0, 0)),
        out_shape=jax.ShapeDtypeStruct(many(depth), f32),
        scratch_shapes=[y_scratch],
        name="forward_y",
    )(*y_tables, early)

    def swap(field):
        return lax.all_to_all(field, "row", split_axis=0, concat_axis=0, tiled=True)

    outgoing, _ = lax.optimization_barrier((outgoing, mine[0]))
    arrived = swap(outgoing)

    block = groups * pair

    small = groups * SUB
    lead = lambda: lax.broadcasted_iota(jnp.int32, (SUB, lanes), 0)

    steps = tiles // 2

    def per_step(n, count):
        return pltpu.VMEM((count, n * block, 2 * lanes), f32)

    def project_kernel(wx_any, wxi_any, turn_ref, s_ref, a_any, b_any, o_ref,
                       wx_ref, wxi_ref, a_s, b_ref, z_s, t_all, zc_s, sems):
        loads = [pltpu.make_async_copy(wx_any, wx_ref, sems.at[0])]
        for step in range(steps):
            mine_rows = pl.ds(step * pair, pair)
            loads.append(pltpu.make_async_copy(a_any.at[:, :, mine_rows, :], a_s.at[step], sems.at[step + 1]))
        loads.append(pltpu.make_async_copy(b_any, b_ref, sems.at[steps + 1]))
        loads.append(pltpu.make_async_copy(wxi_any, wxi_ref, sems.at[steps + 2]))
        for n in (0, 1, steps + 1, steps + 2, *range(2, steps + 1)):
            loads[n].start()

        def forward(step):
            z, zc, t_s = z_s.at[step], zc_s.at[step], t_all.at[step]
            for d in range(depth):
                for h in range(2):
                    j = step * 2 + h
                    tile = [(s_ref[s, d, j, 0], s_ref[s, d, j, 1]) for s in range(groups)]
                    x_radix(tile, z, d * block + h * SUB, turn_ref, lanes, pair)
                if step == 0 and d == 0:
                    loads[0].wait()
                zc[d * block:(d + 1) * block, :] = data_table(z[d * block:(d + 1) * block, :], wx_ref)
            loads[step + 1].wait()
            for t in range(groups):
                here = slice(t * pair, (t + 1) * pair)
                cols = slice(t * lanes, (t + 1) * lanes)
                re = im = None
                for d in range(depth):
                    at = slice(d * block + t * pair, d * block + (t + 1) * pair)
                    zr, zi = zc[at, :lanes], zc[at, lanes:]
                    kr, ki = a_s[step, 0, d, :, cols], a_s[step, 1, d, :, cols]
                    re = plus(re, zr * kr - zi * ki)
                    im = plus(im, zr * ki + zi * kr)
                t_s[here, :lanes] = re
                t_s[here, lanes:] = im

        def packed():
            z, zc, t_s = z_s.at[steps], zc_s.at[steps], t_all.at[0]

            def row(s, c):
                out = s_ref[s, 0, 0, c, 0:1, :]
                for d in range(1, depth):
                    out = jnp.where(lead() == d, s_ref[s, d, 0, c, 0:1, :], out)
                return jnp.broadcast_to(out, (SUB, lanes))

            x_radix([(row(s, 0), -row(s, 1)) for s in range(groups)], z, 0, turn_ref, lanes, SUB)
            zc[:small, :] = data_table(z[:small, :], wx_ref)
            loads[steps + 1].wait()
            for t in range(groups):
                at = slice(t * SUB, (t + 1) * SUB)
                cols = slice(t * lanes, (t + 1) * lanes)
                zr, zi = zc[at, :lanes], zc[at, lanes:]
                kr, ki = b_ref[0, :, cols], b_ref[1, :, cols]
                top = slice(t * pair, t * pair + 1)
                t_s[top, :lanes] += jnp.sum(zr * kr - zi * ki, axis=0, keepdims=True)
                t_s[top, lanes:] += jnp.sum(zr * ki + zi * kr, axis=0, keepdims=True)

        def back(step):
            zc = z_s.at[step]
            zc[:block, :] = data_table(t_all[step], wxi_ref)
            for h in range(2):
                for s, (re, im) in enumerate(x_unradix(zc, h * SUB, turn_ref, groups, lanes, pair)):
                    o_ref[s, step * 2 + h, 0] = re
                    o_ref[s, step * 2 + h, 1] = im

        forward(0)
        packed()
        loads[steps + 2].wait()
        for step in range(steps):
            if step + 1 < steps:
                forward(step + 1)
            back(step)

    hbm = pl.BlockSpec(memory_space=pl.ANY)
    outgoing = pl.pallas_call(
        project_kernel,
        in_specs=[hbm, hbm, whole(*turn.shape), near, hbm, hbm],
        out_specs=near,
        out_shape=pltpu.VMEM(send_shape, f32),
        scratch_shapes=[pltpu.VMEM(w_x.shape, bf), pltpu.VMEM(w_xi.shape, bf),
                        pltpu.VMEM((steps, 2, depth, pair, length), f32), pltpu.VMEM((2, SUB, length), f32),
                        per_step(depth, steps + 1), per_step(1, steps), per_step(depth, steps + 1),
                        pltpu.SemaphoreType.DMA((steps + 3,))],
        compiler_params=pltpu.CompilerParams(vmem_limit_bytes=36 << 20),
        name="project_x",
    )(far(w_x), far(w_xi), turn, keep(arrived), far(a_all), far(b_all))
    arrived = swap(outgoing)

    def ratio_kernel(wy_ref, w0_ref, turn_ref, g_ref, bg_ref, me_ref, p_ref, o_ref, z):
        def fetch(t):
            return g_ref[:, t].reshape(groups * 2 * SUB, rows)

        def write(here, outs):
            ratio = []
            for a, value in enumerate(outs):
                cols = slice(a * lanes, (a + 1) * lanes)
                p_ref[here, cols] = value
                ratio.append(me_ref[here, cols] / jnp.maximum(value + bg_ref[here, cols], FLOOR))
            y_store(ratio, z, here, turn_ref, groups, lanes)

        y_inverse(fetch, write, z, wy_ref, w0_ref, turn_ref, groups, rows, lanes)
        for t in range(tiles):
            out = table_data(w0_ref if t == 0 else wy_ref, z[t])
            o_ref[:, t] = out.reshape(groups, 2, SUB, rows)

    projection, outgoing = pl.pallas_call(
        ratio_kernel,
        in_specs=[near] * 6,
        out_specs=[whole(rows, length), near],
        out_shape=[jax.ShapeDtypeStruct((rows, length), f32), pltpu.VMEM(send_shape, f32)],
        scratch_shapes=[y_scratch],
        compiler_params=pltpu.CompilerParams(vmem_limit_bytes=16 << 20),
        name="ratio",
    )(*y_near, keep(arrived), keep(background), keep(measured))
    arrived = swap(outgoing)

    def correct_kernel(wx_ref, wxi_ref, turn_ref, s_ref, a_ref, b_ref, o_ref, z_s, zq_s, zc_s, cs_s):
        def forward(step):
            z, zq, c_s = z_s.at[step], zq_s.at[step], cs_s.at[step]
            for h in range(2):
                j = step * 2 + h
                tile = [(s_ref[s, j, 0], s_ref[s, j, 1]) for s in range(groups)]
                x_radix(tile, z, h * SUB, turn_ref, lanes, pair)
            zq[...] = data_table(z[...], wx_ref)
            mine_rows = slice(step * pair, (step + 1) * pair)
            for t in range(groups):
                here = slice(t * pair, (t + 1) * pair)
                cols = slice(t * lanes, (t + 1) * lanes)
                zr, zi = zq[here, :lanes], zq[here, lanes:]
                for d in range(depth):
                    at = slice(d * block + t * pair, d * block + (t + 1) * pair)
                    kr, ki = a_ref[0, d, mine_rows, cols], a_ref[1, d, mine_rows, cols]
                    c_s[at, :lanes] = zr * kr + zi * ki
                    c_s[at, lanes:] = zi * kr - zr * ki

        def packed():
            z, zq, c_s = z_s.at[steps], zq_s.at[steps], cs_s.at[0]
            tile = [(s_ref[s, 0, 0], -s_ref[s, 0, 1]) for s in range(groups)]
            x_radix(tile, z, 0, turn_ref, lanes, SUB)
            zq[:small, :] = data_table(z[:small, :], wx_ref)
            for t in range(groups):
                at = slice(t * SUB, t * SUB + 1)
                cols = slice(t * lanes, (t + 1) * lanes)
                zr, zi = zq[at, :lanes], zq[at, lanes:]
                kr, ki = b_ref[0, :, cols], b_ref[1, :, cols]
                re, im = zr * kr + zi * ki, zi * kr - zr * ki
                for d in range(depth):
                    top = slice(d * block + t * pair, d * block + t * pair + 1)
                    c_s[top, :lanes] += re[d:d + 1, :]
                    c_s[top, lanes:] += im[d:d + 1, :]

        def back(step):
            zc, c_s = zc_s.at[step], cs_s.at[step]
            for d in range(depth):
                zc[d * block:(d + 1) * block, :] = data_table(c_s[d * block:(d + 1) * block, :], wxi_ref)
                for h in range(2):
                    out = x_unradix(zc, d * block + h * SUB, turn_ref, groups, lanes, pair)
                    for s, (re, im) in enumerate(out):
                        o_ref[s, d, step * 2 + h, 0] = re
                        o_ref[s, d, step * 2 + h, 1] = im

        forward(0)
        packed()
        for step in range(steps):
            if step + 1 < steps:
                forward(step + 1)
            back(step)

    outgoing = pl.pallas_call(
        correct_kernel,
        in_specs=[near] * 6,
        out_specs=near,
        out_shape=pltpu.VMEM(many(depth), f32),
        scratch_shapes=[per_step(1, steps + 1), per_step(1, steps + 1), per_step(depth, steps), per_step(depth, steps)],
        compiler_params=pltpu.CompilerParams(vmem_limit_bytes=32 << 20),
        name="correct_x",
    )(*x_near, keep(arrived), keep(a_all), keep(b_all))
    arrived = swap(outgoing)

    def final_kernel(wy_ref, w0_ref, turn_ref, g_ref, v_ref, o_ref, z, out_s, sems):
        def product(d, t):
            spectrum = g_ref[:, d, t].reshape(groups * 2 * SUB, rows)
            z[d % 2, t] = data_table(spectrum.T, w0_ref if t == 0 else wy_ref)

        def lines(d, first, last):
            for i in range(first, last):
                here = slice(i * SUB, (i + 1) * SUB)
                for a, value in enumerate(c2r(y_load(z.at[d % 2], here, turn_ref, groups, lanes))):
                    cols = slice(a * lanes, (a + 1) * lanes)
                    out_s[d, here, cols] = v_ref[d, here, cols] * value

        copies = []
        share = rows // SUB // tiles
        for t in range(tiles):
            product(0, t)
        for d in range(depth):
            for t in range(tiles):
                if d + 1 < depth:
                    product(d + 1, t)
                lines(d, t * share, (t + 1) * share)
            copies.append(pltpu.make_async_copy(out_s.at[d], o_ref.at[d], sems.at[d]))
            copies[d].start()
        for copy in copies:
            copy.wait()

    new_volume = pl.pallas_call(
        final_kernel,
        in_specs=[near] * 5,
        out_specs=pl.BlockSpec(memory_space=pl.ANY),
        out_shape=pltpu.HBM((depth, rows, length), f32),
        scratch_shapes=[pltpu.VMEM((2, tiles, rows, 2 * lanes), f32),
                        pltpu.VMEM((depth, rows, length), f32), pltpu.SemaphoreType.DMA((depth,))],
        compiler_params=pltpu.CompilerParams(vmem_limit_bytes=16 << 20),
        name="final_y",
    )(*y_near, keep(arrived), keep(volume))
    return new_volume, projection


def solution(mesh):
    groups, parts = mesh.shape["row"], mesh.shape["vol"]

    def shards(volume, psf_spectra, background, measured):
        rows = volume.shape[1]
        fits = parts == 2 and rows == LANES and rows == SUB * groups
        body = fast_shards if fits else generic_shards
        return body(volume, psf_spectra, background, measured)

    in_specs = (
        P("vol", "row", None),
        P(None, None, "row", None),
        P("row", None),
        P(("vol", "row"), None),
    )
    out_specs = (P("vol", "row", None), P(("vol", "row"), None))
    return jax.shard_map(shards, mesh=mesh, in_specs=in_specs, out_specs=out_specs, check_vma=False)
```
